32 devices in a mesh: dp: 8 (over z, y), tensor: 4 (over x, core).
Axes of the slice: x: 2, y: 2, z: 4, core: 2. Of those that a mesh axis runs over, the one named last changes fastest.
Arguments:
- attn_out: bfloat16 [1280, 2048], P('dp', 'tensor'), may hold values from -6 to 6
- residual: bfloat16 [1280, 2048], P(('dp', 'tensor')), may hold values from -6 to 6
- out_weight: bfloat16 [2048, 2048], P('tensor'), may hold values from -0.125 to 0.125
- norm_gain: float32 [2048], replicated, may hold values from 0.25 to 1.75
- router_weight: bfloat16 [2048, 64], replicated, may hold values from -0.125 to 0.125
- routes: int32 [1280, 8], P(('dp', 'tensor')), may hold values from 0 to 63, all different within a row; in each aligned block of 40 rows (0 to 39, 40 to 79, ...) at most 8 rows name the same one
- gate_up: bfloat16 [64, 2048, 2, 1024], P('dp', None, None, 'tensor'), may hold values from -0.125 to 0.125
- down_weight: bfloat16 [64, 1024, 2048], P('dp', 'tensor'), may hold values from -0.1875 to 0.1875
- final_gain: float32 [2048], replicated, may hold values from 0.25 to 1.75
- kv_pages: bfloat16 [256, 16, 16, 256], P('dp', None, 'tensor'), may hold values from -6 to 6
- page_pick: int32 [8, 2], P('dp'), may hold values from 0 to 31
- destination: int32 [8, 2], P('dp'), may hold values from 0 to 7, as said below
Outputs:
- new_residual: bfloat16 [1280, 2048], P(('dp', 'tensor'))
- normed: bfloat16 [1280, 2048], P(('dp', 'tensor'))
- arrived: bfloat16 [16, 16, 16, 256], P('dp', None, 'tensor')
The draws below stay inside these ranges and needn't reach their ends.
Inputs may be any that keep to these rules, and one draw needn't show every extreme that they name: `routes`: each row names 8 different experts; within the rows of one device (aligned blocks of 40 rows) no expert is named by more than 8 rows. `destination`: each column is a permutation of the indices of dp.
All inputs are finite; a program needn't handle non-finite values.
Results may differ from the reference program's by a relative error of at most 0.02.
Values may be sent and summed in bfloat16 or wider, within the bound.
A program may use at most 192 MiB of HBM per device.

```python
import math
import jax
import jax.numpy as jnp
import numpy as np
from jax import lax

D = 2048
HEADS = 16
HD = 128
EXPERTS = 64
FF = 1024
TOPK = 8
TOKQ = 40
CAP = 8
PAGE = 16
PAGES = 32
MIG = 2
TOKENS = 1280
N_DP = 8
N_TENSOR = 4


def force_entry(column, source, target):
    iota = jnp.arange(N_DP, dtype=jnp.int32)
    current = jnp.sum(jnp.where(iota == source, column, 0)).astype(jnp.int32)
    column = jnp.where(column == target, current, column)
    column = jnp.where(iota == source, target, column)
    return column.astype(jnp.int32)


def draw_destination(key, part):
    columns = []
    for slot_number in range(MIG):
        column = jax.random.permutation(jax.random.fold_in(key, 11 + slot_number), N_DP).astype(jnp.int32)
        start = jax.random.randint(jax.random.fold_in(key, 101 + slot_number), (), 0, N_DP).astype(jnp.int32)
        if slot_number % 2 == 0:
            column = force_entry(column, start, (start + N_DP // 2) % N_DP)
        else:
            column = force_entry(column, start, (start + 1) % N_DP)
            column = force_entry(column, (start + 3) % N_DP, (start + 2) % N_DP)
        columns.append(column)
    return jnp.stack(columns, axis=1).astype(jnp.int32)


def place_ends(entries, stream_key, smallest, high):
    longest = entries.shape.index(max(entries.shape))
    spots = []
    for shift in (0, 1):
        where = [jax.random.randint(jax.random.fold_in(stream_key, axis), (), 0, length) for axis, length in enumerate(entries.shape)]
        where[longest] = (where[longest] + shift) % entries.shape[longest]
        spots.append(tuple(where))
    return entries.at[spots[0]].set(smallest).at[spots[1]].set(high)


def shard_levels(key, shape, split, least, top_value):
    gain, own = 1.0, jax.random.fold_in(key, 6)
    for position, parts in split:
        draws = jnp.exp(jax.random.uniform(jax.random.fold_in(own, position), (parts,), jnp.float32, least / len(split), top_value / len(split)))
        gain = gain * jnp.repeat(draws, shape[position] // parts).reshape([-1 if axis == position else 1 for axis in range(len(shape))])
    return gain


def assign_block(rng, own, number, rows, count, top, bound, lean):
    ranking = jax.random.permutation(rng, count)
    heavy_load, common = load_shares(count, rows * top, bound, lean, True), load_shares(count, rows * top, bound, lean, False)
    places = jnp.arange(count)

    def named(lengths, rotation):
        used = int((lengths > 0).sum())
        fixed = max(1, used // 4)
        moved = fixed + (places - fixed + rotation * (used - fixed)) % max(1, count - fixed)
        return jnp.zeros((count,), jnp.int32).at[ranking[jnp.where(places < fixed, places, moved)]].set(jnp.asarray(lengths, jnp.int32))

    lengths = jnp.where(number % 4 == 0, named(heavy_load, number // 4), named(common, number - number // 4 - 1))
    mixed = jax.random.permutation(jax.random.fold_in(own, 3), count)
    donor, taker = mixed[0:count // 2 * 2:2], mixed[1:count // 2 * 2:2]
    room = jnp.minimum(lengths[donor] - 1, bound - lengths[taker]) // 2
    room = jnp.where((donor == ranking[0]) | (taker == ranking[0]) | (lengths[taker] == 0), 0, jnp.maximum(room, 0))
    moved = jax.random.randint(jax.random.fold_in(own, 4), (count // 2,), 0, 1 << 20) % (room + 1)
    lengths = lengths.at[donor].add(-moved).at[taker].add(moved)
    labels = jnp.searchsorted(jnp.cumsum(lengths), jnp.arange(rows * top), side="right").astype(jnp.int32)
    listing = labels.reshape(top, rows).T
    listing = listing[jax.random.permutation(jax.random.fold_in(own, 1), rows)]
    rotation = jax.random.randint(jax.random.fold_in(own, 2), (rows, 1), 0, top)
    return jnp.take_along_axis(listing, (jnp.arange(top)[None, :] + rotation) % top, axis=1)


def load_shares(amount, total, bound, skew, full):
    weights = [(1 << 20) // math.isqrt(grade ** skew) + 1 for grade in range(1, amount + 1)]
    largest = bound if full else min(bound, max(-(-total // amount), total * weights[0] // sum(weights)))
    least = 1 if total - largest >= amount - 1 else 0
    holding, rest = [largest] + [least] * (amount - 1), total - largest - least * (amount - 1)
    while rest > 0:
        candidates = [i for i in range(1, amount) if holding[i] < largest] or [i for i in range(1, amount) if holding[i] < bound]
        mass, budget = sum([weights[i] for i in candidates]), rest
        for i in candidates:
            more = min(bound - holding[i], max(1, budget * weights[i] // mass), rest)
            holding[i] = holding[i] + more
            rest = rest - more
    return np.array(holding)


def normal_values(stream_key, dims, deviation, reach, cuts=(), held_as=jnp.bfloat16):
    factor_of = shard_levels(stream_key, dims, cuts, -0.22, 0.18) if cuts else 1.0
    result = jax.random.normal(stream_key, dims, jnp.float32) * deviation * factor_of
    return jnp.minimum(jnp.maximum(result, -reach), reach).astype(held_as)


def setup_inputs(seed: int = 0) -> dict:
    key_of = jax.random.split(jax.random.key(seed), 13)
    attn_out = normal_values(key_of[0], (TOKENS, HEADS * HD), 1.0, 6.0, ((0, 8), (1, 4)))
    residual = normal_values(key_of[1], (TOKENS, D), 1.0, 6.0, ((0, 32),))
    out_weight = normal_values(key_of[2], (HEADS * HD, D), (HEADS * HD) ** -0.5, 0.125, ((0, 4),))
    norm_gain = jnp.clip(1.0 + 0.15 * jax.random.normal(key_of[3], (D,), jnp.float32), 0.25, 1.75)
    router_weight = normal_values(key_of[4], (D, EXPERTS), D ** -0.5, 0.125)
    routes_keys = jax.random.split(jax.random.fold_in(key_of[5], 1), TOKENS // TOKQ)
    routes_turns = jax.random.permutation(jax.random.fold_in(key_of[5], 3), TOKENS // TOKQ)
    routes = jax.vmap(lambda own, number: assign_block(jax.random.fold_in(key_of[5], 2), own, number, TOKQ, EXPERTS, TOPK, CAP, 2))(routes_keys, routes_turns).reshape((TOKENS, TOPK))
    gate_up = normal_values(key_of[6], (EXPERTS, D, 2, FF), D ** -0.5, 0.125, ((0, 8), (3, 4)))
    down_weight = normal_values(key_of[7], (EXPERTS, FF, D), FF ** -0.5, 0.1875, ((0, 8), (1, 4)))
    final_gain = jnp.clip(1.0 + 0.15 * jax.random.normal(key_of[8], (D,), jnp.float32), 0.25, 1.75)
    kv_pages = normal_values(key_of[9], (N_DP * PAGES, PAGE, HEADS, 2 * HD), 1.0, 6.0, ((0, 8), (2, 4)))
    page_pick = place_ends(jax.random.randint(key_of[10], (N_DP, MIG), 0, PAGES), jax.random.fold_in(key_of[10], 1), 0, PAGES - 1).astype(jnp.int32)
    destination = draw_destination(jax.random.fold_in(key_of[12], 71), 0)
    return dict(attn_out=attn_out, residual=residual, out_weight=out_weight, norm_gain=norm_gain, router_weight=router_weight, routes=routes, gate_up=gate_up, down_weight=down_weight, final_gain=final_gain, kv_pages=kv_pages, page_pick=page_pick, destination=destination)


def rms_scale(values, gain_vec):
    mean_sq = lax.optimization_barrier(jnp.mean(values * values, axis=-1, keepdims=True))
    return values * lax.rsqrt(mean_sq + 1e-06) * gain_vec

def reference(attn_out, residual, out_weight, norm_gain, router_weight, routes, gate_up, down_weight, final_gain, kv_pages, page_pick, destination):
    projected = jnp.dot(attn_out, out_weight, preferred_element_type=jnp.float32)
    mixed_sum = residual.astype(jnp.float32) + projected
    normed_in = rms_scale(mixed_sum, norm_gain).astype(jnp.bfloat16)
    logits = jnp.dot(normed_in, router_weight, preferred_element_type=jnp.float32)
    picked = jnp.take_along_axis(logits, routes, axis=1)
    gate_values = jax.nn.sigmoid(picked).astype(jnp.bfloat16)
    expert_iota = jnp.arange(EXPERTS, dtype=jnp.int32)
    onehot = (routes[:, :, None] == expert_iota[None, None, :]).astype(jnp.float32)
    gate_table = jnp.einsum('tk,tke->te', gate_values.astype(jnp.float32), onehot)
    most_rows = min(TOKENS, N_DP * N_TENSOR * CAP)
    row_iota = jnp.arange(most_rows, dtype=jnp.int32)

    def one_expert(running, inputs):
        expert_index, paired_weight, down_mat = inputs
        routed = jnp.any(routes == expert_index, axis=1)
        routed_count = jnp.sum(routed.astype(jnp.int32))
        positions = jnp.nonzero(routed, size=most_rows, fill_value=0)[0].astype(jnp.int32)
        valid = (row_iota < routed_count).astype(jnp.float32)
        weight = gate_table[positions, expert_index] * valid
        expert_rows = normed_in[positions].astype(jnp.float32)
        paired = jnp.einsum('md,dgf->mgf', expert_rows, paired_weight.astype(jnp.float32))
        hidden = (jax.nn.silu(paired[:, 0, :]) * paired[:, 1, :]).astype(jnp.bfloat16)
        expert_out = jnp.dot(hidden, down_mat, preferred_element_type=jnp.float32).astype(jnp.bfloat16)
        running = running.at[positions].add(weight[:, None] * expert_out.astype(jnp.float32))
        return (running, None)
    initial = jnp.zeros((TOKENS, D), jnp.float32)
    moe_sum, _ = lax.scan(one_expert, initial, (expert_iota, gate_up, down_weight))
    combined = mixed_sum + moe_sum
    new_residual = combined.astype(jnp.bfloat16)
    normed = rms_scale(combined, final_gain).astype(jnp.bfloat16)
    slot_iota = jnp.arange(MIG, dtype=jnp.int32)
    sources = (jnp.arange(N_DP, dtype=jnp.int32)[:, None] * PAGES + page_pick).reshape(-1).astype(jnp.int32)
    targets = (destination * MIG + slot_iota[None, :]).reshape(-1).astype(jnp.int32)
    arrived = jnp.zeros((N_DP * MIG,) + kv_pages.shape[1:], kv_pages.dtype).at[targets].set(kv_pages[sources])
    return (new_residual, normed, arrived)
```

```python
import jax
import jax.numpy as jnp
from jax import lax
from jax.experimental import pallas as pl
from jax.experimental.pallas import tpu as pltpu
from jax.sharding import PartitionSpec as P

CAP = 8


def rms_scale(values, gain_vec):
    mean_sq = jnp.mean(values * values, axis=-1, keepdims=True)
    return values * lax.rsqrt(mean_sq + 1e-06) * gain_vec


MESH = pl.DeviceIdType.MESH
EXTRA = 128
F32, BF16 = jnp.float32, jnp.bfloat16


def wide(value):
    return value.astype(F32)


class Place:
    def __init__(self):
        group, shard = lax.axis_index("dp"), lax.axis_index("tensor")
        z, y, x, c = group // 2, group % 2, shard // 2, shard % 2
        self.group, self.z, self.y, self.x, self.c = group, z, y, x, c
        self.planes = [z, z + 1 - 2 * (z % 2), (z + 2) % 4, 3 - z]
        self.core_peer = (group, x * 2 + 1 - c)
        self.x_peer = (group, (1 - x) * 2 + c)
        self.y_peer = (z * 2 + 1 - y, shard)
        self.z_peers = [None] + [(plane * 2 + y, shard) for plane in self.planes[1:]]

    def enter(self):
        barrier = pltpu.get_barrier_semaphore()
        peers = [self.core_peer, self.x_peer, self.y_peer] + self.z_peers[1:]
        for peer in peers:
            pl.semaphore_signal(barrier, inc=1, device_id=peer, device_id_type=MESH)
        pl.semaphore_wait(barrier, len(peers))


def sender(send_sems, recv_sems):
    used = []

    def send(source, target, peer):
        index = len(used)
        copy = pltpu.make_async_remote_copy(
            src_ref=source,
            dst_ref=target,
            send_sem=send_sems.at[index],
            recv_sem=recv_sems.at[index],
            device_id=peer,
            device_id_type=MESH,
        )
        copy.start()
        used.append(copy)
        return copy

    return send, used


def block_kernel(
    pick_ref, target_ref,
    attn_hbm, weight_hbm, residual_hbm, gain_hbm, router_hbm, routes_hbm,
    paired_hbm, down_hbm, last_gain_hbm, kv_hbm,
    new_ref, normed_ref, arrived_ref,
    attn, weight, residual, gain, router, routes, staged, paired, down, last_gain, kv,
    made, core_in, x_out, x_in, mixed_ref, everything, slots, combine,
    peer_in, first_out, first_in, second_out, second_in, z_out, z_in, pages_in,
    local_sems, stage_sems, send_sems, recv_sems,
):
    at = Place()
    z, y, x, c, planes = at.z, at.y, at.x, at.c, at.planes
    rows, width = residual.shape
    half = width // 2
    experts = paired.shape[0]
    units = down.shape[1]
    loads = {}
    for index, (name, source, target) in enumerate((
        ("attn", attn_hbm, attn), ("weight", weight_hbm, weight), ("kv", kv_hbm, kv),
        ("residual", residual_hbm, residual), ("gain", gain_hbm, gain),
        ("router", router_hbm, router), ("routes", routes_hbm, routes),
        ("last_gain", last_gain_hbm, last_gain), ("down", down_hbm, down),
    )):
        loads[name] = pltpu.make_async_copy(source, target, local_sems.at[index])

    def stage(e):
        return pltpu.make_async_copy(paired_hbm.at[e], staged.at[e % 2], stage_sems.at[e % 2])

    for name in ("attn", "weight", "kv", "residual", "gain", "router", "routes"):
        loads[name].start()
    stage(0).start()
    stage(1).start()
    loads["last_gain"].start()
    loads["down"].start()

    def split_pairs(e):
        stage(e).wait()

        def piece(i, carry):
            spot = pl.ds(pl.multiple_of(i * 128, 128), 128)
            both = jnp.swapaxes(staged[e % 2, spot], 0, 1)
            paired[e, spot, :units] = both[0]
            paired[e, spot, units:] = both[1]
            return carry

        lax.fori_loop(0, width // 128, piece, 0)
        if e + 2 < experts:
            stage(e + 2).start()

    at.enter()
    send, used = sender(send_sems, recv_sems)

    loads["kv"].wait()
    for slot in range(2):
        pages_in[z, y, slot, pl.ds(0, 16)] = kv[pick_ref[0, slot]]
        pages_in[z, y, slot, 16] = jnp.full(kv.shape[2:], target_ref[0, slot], jnp.int32).astype(
            F32
        ).astype(BF16)
    own_pages = pages_in.at[z, y]
    page_z = [None] + [send(own_pages, own_pages, at.z_peers[j]) for j in (1, 2, 3)]
    page_y = [send(own_pages, own_pages, at.y_peer)]

    loads["attn"].wait()
    loads["weight"].wait()
    halves = [pl.ds(0, half), pl.ds(half, half)]
    far, near, to_x = [], [], []
    for h in (0, 1):
        for start in range(h * half, h * half + half, 512):
            part = jnp.dot(
                attn[...], weight[:, start : start + 512], preferred_element_type=F32
            )
            for shard in range(4):
                made[shard, :, start : start + 512] = part[
                    shard * rows : (shard + 1) * rows
                ].astype(BF16)
        far.append(
            send(made.at[(1 - x) * 2 + 1 - c, :, halves[h]], core_in.at[0, :, halves[h]], at.core_peer)
        )
    for h in (0, 1):
        near.append(
            send(made.at[x * 2 + 1 - c, :, halves[h]], core_in.at[1, :, halves[h]], at.core_peer)
        )
    for h in (0, 1):
        far[h].wait_recv()
        x_out[:, halves[h]] = (
            wide(made[(1 - x) * 2 + c, :, halves[h]]) + wide(core_in[0, :, halves[h]])
        ).astype(BF16)
        to_x.append(send(x_out.at[:, halves[h]], x_in.at[:, halves[h]], at.x_peer))
    for j in (1, 2, 3):
        page_z[j].wait_recv()
        spot = pages_in.at[planes[j], y]
        page_y.append(send(spot, spot, at.y_peer))
    for e in range(EARLY):
        split_pairs(e)
    loads["residual"].wait()
    for h in (0, 1):
        near[h].wait_recv()
        mixed_ref[:, halves[h]] = (
            wide(residual[:, halves[h]])
            + wide(made[x * 2 + c, :, halves[h]])
            + wide(core_in[1, :, halves[h]])
        )
    loads["gain"].wait()
    loads["router"].wait()
    loads["routes"].wait()
    count = router.shape[0]
    named = routes[...]
    expert = lax.broadcasted_iota(jnp.int32, (count, rows), 0)
    hits_t = jnp.zeros((count, rows), F32)
    for k in range(named.shape[0]):
        hits_t = hits_t + jnp.where(named[k : k + 1, :] == expert, 1.0, 0.0)
    later = lax.broadcasted_iota(jnp.int32, (rows, rows), 0)
    sooner = lax.broadcasted_iota(jnp.int32, (rows, rows), 1)
    eye = jnp.where(later == sooner, 1.0, 0.0).astype(BF16)
    over_last = (((1,), (1,)), ((), ()))
    hits = lax.dot_general(eye, hits_t.astype(BF16), over_last, preferred_element_type=F32)
    to_x[0].wait_recv()
    to_x[1].wait_recv()
    mixed = mixed_ref[...] + wide(x_in[...])
    mixed_ref[...] = mixed
    mean_sq = jnp.mean(mixed * mixed, axis=-1, keepdims=True)
    rounded = (mixed * lax.rsqrt(mean_sq + 1e-06) * gain[...]).astype(BF16)
    everything[z, y, x, c, :, :width] = rounded
    logits = lax.dot_general(rounded, router[...], over_last, preferred_element_type=F32)
    gates = jax.nn.sigmoid(logits)
    everything[z, y, x, c, :, width:] = jnp.concatenate([gates * hits, hits], axis=1).astype(BF16)

    columns = [pl.ds(0, half), pl.ds(half, half + EXTRA)]
    first_peer, second_peer = [at.y_peer, at.x_peer], [at.x_peer, at.y_peer]

    def block(h, j, first_other, second_other):
        ys = first_other if h == 0 else second_other
        xs = second_other if h == 0 else first_other
        return everything.at[
            planes[j], 1 - y if ys else y, 1 - x if xs else x, c, :, columns[h]
        ]

    z_copies, first_copies, second_copies = {}, {}, {}
    core_copies = {j: [] for j in range(4)}
    sent = {j: [] for j in range(4)}

    def note(j, copy):
        sent[j].append(copy)
        return copy

    def core(j, spot):
        core_copies[j].append(note(j, send(spot, spot, at.core_peer)))

    def send_z(j):
        for h in (0, 1):
            spot = block(h, 0, 0, 0)
            z_copies[h, j] = note(0, send(spot, spot, at.z_peers[j]))

    def spread(j):
        for h in (0, 1):
            if j:
                z_copies[h, j].wait_recv()
            spot = block(h, j, 0, 0)
            first_copies[h, j] = note(j, send(spot, spot, first_peer[h]))
        for h in (0, 1):
            spot = block(h, j, 0, 0)
            second_copies[h, j, 0] = note(j, send(spot, spot, second_peer[h]))
        for h in (0, 1):
            core(j, block(h, j, 0, 0))

    def spread_first(j):
        for h in (0, 1):
            first_copies[h, j].wait_recv()
            spot = block(h, j, 1, 0)
            second_copies[h, j, 1] = note(j, send(spot, spot, second_peer[h]))
        for h in (0, 1):
            core(j, block(h, j, 1, 0))

    def spread_second(j):
        for other in (0, 1):
            for h in (0, 1):
                second_copies[h, j, other].wait_recv()
                core(j, block(h, j, other, 1))

    lanes = 2 * CAP
    span = experts * lanes
    first_expert = at.group * experts
    pick_row = lax.broadcasted_iota(jnp.int32, (2 * count, 2 * span), 0)
    pick_col = lax.broadcasted_iota(jnp.int32, (2 * count, 2 * span), 1)
    wanted_row = first_expert + (pick_col % span) // lanes + (pick_col // span) * count

    def dispatch(j):
        for copy in core_copies[j]:
            copy.wait_recv()

        def one_chip(i, carry):
            total = None
            picker = jnp.where(pick_row == wanted_row, 1.0, 0.0).astype(BF16)
            before = jnp.where(later > sooner, 1.0, 0.0).astype(BF16)
            lane = lax.broadcasted_iota(jnp.int32, (rows, span), 1)
            for core_id in (0, 1):
                spot = everything.at[planes[j], i // 2, i % 2, core_id]
                local = jnp.dot(spot[:, width:], picker, preferred_element_type=F32)
                named_here = local[:, span:]
                rank = jnp.dot(before, named_here.astype(BF16), preferred_element_type=F32)
                table = jnp.where(
                    (named_here > 0.5)
                    & (rank == wide(lane % CAP))
                    & (lane // CAP % 2 == core_id),
                    1.0,
                    0.0,
                )
                combine[j, i, core_id * rows : (core_id + 1) * rows] = table * local[:, :span]
                placed = lax.dot_general(
                    table.astype(BF16),
                    spot[:, :width],
                    (((0,), (0,)), ((), ())),
                    preferred_element_type=F32,
                )
                total = placed if core_id == 0 else total + placed
            packed = total.astype(BF16)
            for e in range(experts):
                slots[e, j, pl.ds(pl.multiple_of(i * lanes, lanes), lanes), :] = packed[
                    e * lanes : (e + 1) * lanes
                ]
            return carry

        lax.fori_loop(0, 4, one_chip, 0)

    def feed(first_plane, count_planes):
        here = pl.ds(first_plane, count_planes)
        seats = slots.shape[2]

        def one_expert(e, carry):
            taken = slots[e, here].reshape(count_planes * seats, width)
            both = jnp.dot(taken, paired[e], preferred_element_type=F32)
            gate, up = both[:, :units], both[:, units:]
            hidden = (gate / (1.0 + jnp.exp(-gate)) * up).astype(BF16)
            for start in range(0, width, 512):
                out = jnp.dot(
                    hidden, down[e, :, start : start + 512], preferred_element_type=F32
                ).astype(BF16)
                slots[e, here, :, start : start + 512] = out.reshape(count_planes, seats, 512)
            return carry

        lax.fori_loop(0, experts, one_expert, 0)

    peer_copies, first_sums, second_sums, z_sums = {}, {}, {}, {}
    orders = ((1, 1), (0, 1), (1, 0), (0, 0))

    def owner(j, fy, fx, core_id, h=None):
        cut = pl.ds(0, width) if h is None else halves[h]
        return (planes[j], 1 - y if fy else y, 1 - x if fx else x, core_id, slice(None), cut)

    def gather_sums(j):
        for copy in sent[j]:
            copy.wait_send()

        def one_chip(i, carry):
            spot = pl.ds(pl.multiple_of(i * lanes, lanes), lanes)
            table = combine[j, i].astype(BF16)
            for start in range(0, width, 512):
                outs = jnp.concatenate(
                    [slots[e, j, spot, start : start + 512] for e in range(experts)], axis=0
                )
                part = jnp.dot(table, outs, preferred_element_type=F32).astype(F32)
                for core_id in (0, 1):
                    everything[planes[j], i // 2, i % 2, core_id, :, start : start + 512] = part[
                        core_id * rows : (core_id + 1) * rows
                    ].astype(BF16)
            return carry

        lax.fori_loop(0, 4, one_chip, 0)
        for fy, fx in orders:
            peer_copies[j, fy, fx] = send(
                everything.at[owner(j, fy, fx, 1 - c)], peer_in.at[j, fy, fx], at.core_peer
            )

    def both_cores(j, fy, fx, h):
        return wide(everything[owner(j, fy, fx, c, h)]) + wide(peer_in[j, fy, fx, :, halves[h]])

    def sum_first(j):
        for fy, fx in orders[:3]:
            peer_copies[j, fy, fx].wait_recv()
        for second in (1, 0):
            for h in (0, 1):
                fy, fx = (second, 1) if h == 0 else (1, second)
                first_out[j, h, second] = both_cores(j, fy, fx, h).astype(BF16)
                first_sums[j, h, second] = send(
                    first_out.at[j, h, second],
                    first_in.at[j, h, second],
                    (at.x_peer, at.y_peer)[h],
                )

    def sum_second(j):
        for h in (0, 1):
            first_sums[j, h, 1].wait_recv()
            fy, fx = (1, 0) if h == 0 else (0, 1)
            second_out[j, h] = (both_cores(j, fy, fx, h) + wide(first_in[j, h, 1])).astype(BF16)
            second_sums[j, h] = send(
                second_out.at[j, h], second_in.at[j, h], (at.y_peer, at.x_peer)[h]
            )

    def sum_plane(j):
        peer_copies[j, 0, 0].wait_recv()
        for h in (0, 1):
            first_sums[j, h, 0].wait_recv()
            second_sums[j, h].wait_recv()
            total = both_cores(j, 0, 0, h) + wide(first_in[j, h, 0]) + wide(second_in[j, h])
            if j:
                z_out[j - 1, h] = total.astype(BF16)
                z_sums[j, h] = send(z_out.at[j - 1, h], z_in.at[j - 1, h], at.z_peers[j])
            else:
                mixed_ref[:, halves[h]] = mixed_ref[:, halves[h]] + total

    def pages_out():
        for copy in page_y:
            copy.wait_recv()
        me = at.group.astype(F32)
        for slot in range(2):
            found = jnp.zeros(arrived_ref.shape[1:], F32)
            for zs in range(4):
                for ys in (0, 1):
                    held = wide(pages_in[zs, ys, slot])
                    found = found + jnp.where(held[16:17] == me, held[:16], 0.0)
            arrived_ref[slot] = found.astype(BF16)

    def finish():
        loads["last_gain"].wait()
        total_sq = jnp.zeros((rows, 1), F32)
        for h in (0, 1):
            value = mixed_ref[:, halves[h]]
            for j in (3, 2, 1):
                z_sums[j, h].wait_recv()
                value = value + wide(z_in[j - 1, h])
            mixed_ref[:, halves[h]] = value
            total_sq = total_sq + jnp.sum(value * value, axis=-1, keepdims=True)
        scale = lax.rsqrt(total_sq / width + 1e-06)
        for h in (0, 1):
            value = mixed_ref[:, halves[h]]
            new_ref[:, halves[h]] = value.astype(BF16)
            normed_ref[:, halves[h]] = (value * scale * last_gain[:, halves[h]]).astype(BF16)

    steps = dict(
        z=send_z, spread=spread, first=spread_first, second=spread_second, dispatch=dispatch,
        split=split_pairs, feed=feed, down=loads["down"].wait, sums=gather_sums, one=sum_first,
        two=sum_second, plane=sum_plane, pages=pages_out, finish=finish,
    )
    for name, *given in SCHEDULE:
        steps[name](*given)
    waited = {id(copy) for j in range(4) for copy in sent[j]}
    for copy in used:
        if id(copy) not in waited:
            copy.wait_send()


EARLY = 4
SCHEDULE = (
    ("z", 1), ("spread", 0), ("z", 2), ("z", 3),
    ("split", 4), ("spread", 1), ("first", 0),
    ("split", 5), ("second", 0), ("spread", 2), ("first", 1), ("dispatch", 0),
    ("split", 6), ("second", 1), ("spread", 3), ("first", 2), ("dispatch", 1),
    ("split", 7), ("second", 2), ("first", 3), ("dispatch", 2),
    ("second", 3), ("down",), ("pages",), ("dispatch", 3),
    ("feed", 0, 4),
    ("sums", 3), ("sums", 2), ("one", 3), ("sums", 1), ("one", 2), ("two", 3),
    ("sums", 0), ("one", 1), ("two", 2), ("plane", 3),
    ("one", 0), ("two", 1), ("plane", 2), ("two", 0), ("plane", 1), ("plane", 0),
    ("finish",),
)
COPIES = 3 + 4 + 6 + 2 * (3 + 4 + 8 + 16) + 16 + 16 + 8 + 6


def whole_block(
    attn_out, out_weight, residual, norm_gain, router_weight, routes, gate_up, down_weight,
    final_gain, kv_pages, page_pick, destination,
):
    rows, width = residual.shape
    half = width // 2
    experts, _, _, units = gate_up.shape
    hbm, smem, vmem = (
        pl.BlockSpec(memory_space=space) for space in (pl.ANY, pltpu.SMEM, pltpu.VMEM)
    )
    scratch = lambda value: pltpu.VMEM(value.shape, value.dtype)
    blocks = lambda *shape: pltpu.VMEM(shape, BF16)
    page = kv_pages.shape[1:]
    gain, last_gain = norm_gain.reshape(1, width), final_gain.reshape(1, width)
    router, named = router_weight.T, routes.T
    return pl.pallas_call(
        block_kernel,
        out_shape=(jax.ShapeDtypeStruct((rows, width), BF16),) * 2
        + (jax.ShapeDtypeStruct((2,) + page, BF16),),
        in_specs=[smem] * 2 + [hbm] * 10,
        out_specs=(vmem,) * 3,
        scratch_shapes=[
            scratch(attn_out), scratch(out_weight), scratch(residual), scratch(gain),
            scratch(router), scratch(named),
            blocks(2, width, 2, units),
            blocks(experts, width, 2 * units),
            scratch(down_weight), scratch(last_gain), scratch(kv_pages),
            blocks(4, rows, width),
            blocks(2, rows, width),
            blocks(rows, width),
            blocks(rows, width),
            pltpu.VMEM((rows, width), F32),
            blocks(4, 2, 2, 2, rows, width + EXTRA),
            blocks(experts, 4, 4 * 2 * CAP, width),
            pltpu.VMEM((4, 4, 2 * rows, experts * 2 * CAP), F32),
            blocks(4, 2, 2, rows, width),
            blocks(4, 2, 2, rows, half),
            blocks(4, 2, 2, rows, half),
            blocks(4, 2, rows, half),
            blocks(4, 2, rows, half),
            blocks(3, 2, rows, half),
            blocks(3, 2, rows, half),
            blocks(4, 2, 2, page[0] + 1, page[1], page[2]),
            pltpu.SemaphoreType.DMA((9,)),
            pltpu.SemaphoreType.DMA((2,)),
            pltpu.SemaphoreType.DMA((COPIES,)),
            pltpu.SemaphoreType.DMA((COPIES,)),
        ],
        compiler_params=pltpu.CompilerParams(
            collective_id=0, has_side_effects=True, vmem_limit_bytes=60 << 20
        ),
        name="block",
    )(
        page_pick, destination, attn_out, out_weight, residual, gain, router, named,
        gate_up, down_weight, last_gain, kv_pages,
    )


def pair_kernel(taken_ref, paired_ref, out_ref):
    units = paired_ref.shape[3]
    both = jnp.swapaxes(paired_ref[0], 0, 1)
    for part in (0, 1):
        out_ref[0, :, part * units : (part + 1) * units] = jnp.dot(
            taken_ref[0], both[part], preferred_element_type=F32
        )


def pair_products(taken, gate_up):
    experts, count, width = taken.shape
    units = gate_up.shape[3]
    step = 256 if count % 256 == 0 else count
    return pl.pallas_call(
        pair_kernel,
        grid=(experts, count // step),
        out_shape=jax.ShapeDtypeStruct((experts, count, 2 * units), F32),
        in_specs=[
            pl.BlockSpec((1, step, width), lambda e, i: (e, i, 0)),
            pl.BlockSpec((1, width, 2, units), lambda e, i: (e, 0, 0, 0)),
        ],
        out_specs=pl.BlockSpec((1, step, 2 * units), lambda e, i: (e, i, 0)),
        compiler_params=pltpu.CompilerParams(vmem_limit_bytes=32 << 20),
        name="pair",
    )(taken, gate_up)


def migrate(kv_pages, page_pick, destination):
    groups = lax.axis_size("dp")
    chosen_pages = jnp.concatenate(
        [
            lax.dynamic_slice_in_dim(kv_pages, page_pick[0, slot], 1, axis=0)
            for slot in range(page_pick.shape[1])
        ],
        axis=0,
    )
    owners = jnp.arange(groups, dtype=jnp.int32)[:, None] == destination[0][None, :]
    outgoing = jnp.where(
        owners[:, :, None, None, None], chosen_pages[None], jnp.zeros((), kv_pages.dtype)
    )
    incoming = lax.all_to_all(outgoing, "dp", split_axis=0, concat_axis=0, tiled=True)
    return jnp.sum(incoming, axis=0)


def local_slots(routes_all, first, local_experts, groups, shards, rows):
    hits = jnp.any(
        routes_all[:, :, None] == first + jnp.arange(local_experts, dtype=jnp.int32), axis=1
    )
    hits = hits.reshape(groups, shards * rows, local_experts)
    token = jnp.arange(shards * rows, dtype=jnp.int32)
    before = (token[:, None] > token[None, :]) & (
        token[:, None] // rows == token[None, :] // rows
    )
    rank = jnp.einsum(
        "ut,bte->bue",
        before.astype(jnp.bfloat16),
        hits.astype(jnp.bfloat16),
        preferred_element_type=jnp.float32,
    ).astype(jnp.int32)
    within = (token // rows * CAP)[None, :, None] + rank
    within = jnp.where(hits, within, -1)
    slots = jnp.arange(shards * CAP, dtype=jnp.int32)
    table = within[:, :, :, None] == slots
    return table.reshape(groups, shards * rows, local_experts * shards * CAP)


def per_device(
    attn_out,
    residual,
    out_weight,
    norm_gain,
    router_weight,
    routes,
    gate_up,
    down_weight,
    final_gain,
    kv_pages,
    page_pick,
    destination,
):
    groups = lax.axis_size("dp")
    shards = lax.axis_size("tensor")
    rows, width = residual.shape
    local_experts = gate_up.shape[0]
    first = lax.axis_index("dp") * local_experts
    if groups == 8 and shards == 4:
        return whole_block(
            attn_out, out_weight, residual, norm_gain, router_weight, routes, gate_up,
            down_weight, final_gain, kv_pages, page_pick, destination,
        )
    arrived = migrate(kv_pages, page_pick, destination)
    routes_all = lax.all_gather(routes, ("dp", "tensor"), axis=0, tiled=True)
    projected = lax.psum_scatter(
        jnp.dot(attn_out, out_weight, preferred_element_type=jnp.float32).astype(
            jnp.bfloat16
        ),
        "tensor",
        scatter_dimension=0,
        tiled=True,
    ).astype(jnp.float32)
    mixed_sum = residual.astype(jnp.float32) + projected
    normed_in = rms_scale(mixed_sum, norm_gain).astype(jnp.bfloat16)
    tokens = lax.all_gather(normed_in, ("dp", "tensor"), axis=0, tiled=True)
    table = local_slots(routes_all, first, local_experts, groups, shards, rows)
    local_router = lax.dynamic_slice_in_dim(router_weight, first, local_experts, axis=1)
    logits = jnp.dot(tokens, local_router, preferred_element_type=jnp.float32)
    gates = jax.nn.sigmoid(logits).astype(jnp.bfloat16)
    tokens = tokens.reshape(groups, shards * rows, width)
    gates = jnp.repeat(
        gates.reshape(groups, shards * rows, local_experts), shards * CAP, axis=2
    )
    placement = table.astype(jnp.bfloat16)
    combine = jnp.where(table, gates, jnp.zeros((), jnp.bfloat16))
    slotted = jnp.einsum(
        "bts,btd->bsd", placement, tokens, preferred_element_type=jnp.float32
    ).astype(jnp.bfloat16)
    slotted = slotted.reshape(groups, local_experts, shards * CAP, width)
    units = gate_up.shape[3]
    taken = jnp.swapaxes(slotted, 0, 1).reshape(local_experts, -1, width)
    paired = pair_products(taken, gate_up)
    paired = jnp.swapaxes(paired.reshape(local_experts, groups, shards * CAP, 2 * units), 0, 1)
    hidden = (jax.nn.silu(paired[..., :units]) * paired[..., units:]).astype(jnp.bfloat16)
    expert_out = jnp.einsum(
        "becf,efd->becd", hidden, down_weight, preferred_element_type=jnp.float32
    ).astype(jnp.bfloat16)
    expert_out = expert_out.reshape(groups, local_experts * shards * CAP, width)
    partial = jnp.einsum(
        "bts,bsd->btd", combine, expert_out, preferred_element_type=jnp.float32
    ).astype(jnp.bfloat16)
    moe_sum = lax.psum_scatter(
        partial.reshape(groups * shards * rows, width),
        ("dp", "tensor"),
        scatter_dimension=0,
        tiled=True,
    ).astype(jnp.float32)
    combined = mixed_sum + moe_sum
    new_residual = combined.astype(jnp.bfloat16)
    normed = rms_scale(combined, final_gain).astype(jnp.bfloat16)
    return (new_residual, normed, arrived)


def solution(mesh):
    in_specs = (
        P("dp", "tensor"),
        P(("dp", "tensor"), None),
        P("tensor", None),
        P(),
        P(),
        P(("dp", "tensor"), None),
        P("dp", None, None, "tensor"),
        P("dp", "tensor", None),
        P(),
        P("dp", None, "tensor", None),
        P("dp", None),
        P("dp", None),
    )
    out_specs = (
        P(("dp", "tensor"), None),
        P(("dp", "tensor"), None),
        P("dp", None, "tensor", None),
    )
    return jax.shard_map(
        per_device, mesh=mesh, in_specs=in_specs, out_specs=out_specs, check_vma=False
    )
```

```python
import jax
import jax.numpy as jnp
from jax import lax
from jax.experimental import pallas as pl
from jax.experimental.pallas import tpu as pltpu
from jax.sharding import PartitionSpec as P

CAP = 8


def rms_scale(values, gain_vec):
    mean_sq = jnp.mean(values * values, axis=-1, keepdims=True)
    return values * lax.rsqrt(mean_sq + 1e-06) * gain_vec


MESH = pl.DeviceIdType.MESH
EXTRA = 128
F32, BF16 = jnp.float32, jnp.bfloat16


def wide(value):
    return value.astype(F32)


class Place:
    def __init__(self):
        group, shard = lax.axis_index("dp"), lax.axis_index("tensor")
        z, y, x, c = group // 2, group % 2, shard // 2, shard % 2
        self.group, self.z, self.y, self.x, self.c = group, z, y, x, c
        self.planes = [z, z + 1 - 2 * (z % 2), (z + 2) % 4, 3 - z]
        self.core_peer = (group, x * 2 + 1 - c)
        self.x_peer = (group, (1 - x) * 2 + c)
        self.y_peer = (z * 2 + 1 - y, shard)
        self.z_peers = [None] + [(plane * 2 + y, shard) for plane in self.planes[1:]]

    def enter(self):
        barrier = pltpu.get_barrier_semaphore()
        peers = [self.core_peer, self.x_peer, self.y_peer] + self.z_peers[1:]
        for peer in peers:
            pl.semaphore_signal(barrier, inc=1, device_id=peer, device_id_type=MESH)
        pl.semaphore_wait(barrier, len(peers))


def sender(send_sems, recv_sems):
    used = []

    def send(source, target, peer):
        index = len(used)
        copy = pltpu.make_async_remote_copy(
            src_ref=source,
            dst_ref=target,
            send_sem=send_sems.at[index],
            recv_sem=recv_sems.at[index],
            device_id=peer,
            device_id_type=MESH,
        )
        copy.start()
        used.append(copy)
        return copy

    return send, used


def block_kernel(
    pick_ref, target_ref,
    attn_hbm, weight_hbm, residual_hbm, gain_hbm, router_hbm, routes_hbm,
    paired_hbm, down_hbm, kv_hbm,
    combined_ref, arrived_ref,
    attn, weight, residual, gain, router, routes, staged, paired, down, kv,
    made, core_in, x_out, x_in, mixed_ref, everything, slots, combine,
    pick, pick_t, want, want_t, peer_in, first_out, first_in, second_out, second_in, z_out, z_in, pages_in,
    local_sems, stage_sems, send_sems, recv_sems,
):
    at = Place()
    z, y, x, c, planes = at.z, at.y, at.x, at.c, at.planes
    rows, width = residual.shape
    half = width // 2
    experts = paired.shape[0]
    units = down.shape[1]
    loads = {}
    for index, (name, source, target) in enumerate((
        ("attn", attn_hbm, attn), ("weight", weight_hbm, weight), ("kv", kv_hbm, kv),
        ("residual", residual_hbm, residual), ("gain", gain_hbm, gain),
        ("router", router_hbm, router), ("routes", routes_hbm, routes),
        ("down", down_hbm, down),
    )):
        loads[name] = pltpu.make_async_copy(source, target, local_sems.at[index])

    def stage(e):
        return pltpu.make_async_copy(paired_hbm.at[e], staged.at[e % 2], stage_sems.at[e % 2])

    for name in ("attn", "weight", "kv", "residual", "gain", "router", "routes"):
        loads[name].start()
    stage(0).start()
    stage(1).start()
    loads["down"].start()

    def split_pairs(e):
        stage(e).wait()

        def piece(i, carry):
            spot = pl.ds(pl.multiple_of(i * 128, 128), 128)
            both = jnp.swapaxes(staged[e % 2, spot], 0, 1)
            paired[e, spot, :units] = both[0]
            paired[e, spot, units:] = both[1]
            return carry

        lax.fori_loop(0, width // 128, piece, 0)
        if e + 2 < experts:
            stage(e + 2).start()

    at.enter()
    send, used = sender(send_sems, recv_sems)

    loads["kv"].wait()
    for slot in range(2):
        pages_in[z, y, slot, pl.ds(0, 16)] = kv[pick_ref[0, slot]]
        pages_in[z, y, slot, 16] = jnp.full(kv.shape[2:], target_ref[0, slot], jnp.int32).astype(
            F32
        ).astype(BF16)
    own_pages = pages_in.at[z, y]
    page_z = [None] + [send(own_pages, own_pages, at.z_peers[j]) for j in (1, 2, 3)]
    page_y = [send(own_pages, own_pages, at.y_peer)]

    def pass_page(j):
        page_z[j].wait_recv()
        spot = pages_in.at[planes[j], y]
        page_y.append(send(spot, spot, at.y_peer))

    loads["attn"].wait()
    loads["weight"].wait()
    halves = [pl.ds(0, half), pl.ds(half, half)]
    far, near, to_x = [], [], []
    for h in (0, 1):
        for start in range(h * half, h * half + half, 512):
            part = jnp.dot(
                attn[...], weight[:, start : start + 512], preferred_element_type=F32
            )
            for shard in range(4):
                made[shard, :, start : start + 512] = part[
                    shard * rows : (shard + 1) * rows
                ].astype(BF16)
        far.append(
            send(made.at[(1 - x) * 2 + 1 - c, :, halves[h]], core_in.at[0, :, halves[h]], at.core_peer)
        )
    for h in (0, 1):
        near.append(
            send(made.at[x * 2 + 1 - c, :, halves[h]], core_in.at[1, :, halves[h]], at.core_peer)
        )
    for h in (0, 1):
        far[h].wait_recv()
        x_out[:, halves[h]] = (
            wide(made[(1 - x) * 2 + c, :, halves[h]]) + wide(core_in[0, :, halves[h]])
        ).astype(BF16)
        to_x.append(send(x_out.at[:, halves[h]], x_in.at[:, halves[h]], at.x_peer))
    for name, index in WARM:
        {"split": split_pairs, "page": pass_page}[name](index)
    loads["residual"].wait()
    for h in (0, 1):
        near[h].wait_recv()
        mixed_ref[:, halves[h]] = (
            wide(residual[:, halves[h]])
            + wide(made[x * 2 + c, :, halves[h]])
            + wide(core_in[1, :, halves[h]])
        )
    loads["gain"].wait()
    loads["router"].wait()
    loads["routes"].wait()
    count = router.shape[0]
    named = routes[...]
    expert = lax.broadcasted_iota(jnp.int32, (count, rows), 0)
    hits_t = jnp.zeros((count, rows), F32)
    for k in range(named.shape[0]):
        hits_t = hits_t + jnp.where(named[k : k + 1, :] == expert, 1.0, 0.0)
    later = lax.broadcasted_iota(jnp.int32, (rows, rows), 0)
    sooner = lax.broadcasted_iota(jnp.int32, (rows, rows), 1)
    eye = jnp.where(later == sooner, 1.0, 0.0).astype(BF16)
    over_last = (((1,), (1,)), ((), ()))
    hits = lax.dot_general(eye, hits_t.astype(BF16), over_last, preferred_element_type=F32)
    before = jnp.where(later > sooner, 1.0, 0.0).astype(BF16)
    places = hits * (1.0 + jnp.dot(before, hits.astype(BF16), preferred_element_type=F32))
    lanes = 2 * CAP
    span = experts * lanes
    first_expert = at.group * experts

    def iota(shape, axis):
        return lax.broadcasted_iota(jnp.int32, shape, axis)

    def wanted(slot, token):
        return wide(jnp.where(slot // CAP % 2 == token // rows, slot % CAP + 1, -1))

    def picks(slot, entry):
        chosen = first_expert + slot % span // lanes + slot // span * count
        return jnp.where(chosen == entry, 1.0, 0.0).astype(BF16)

    tall, square = (2 * span, 2 * count), (span, 2 * rows)
    pick_t[...] = picks(iota(tall, 0), iota(tall, 1))
    pick[...] = picks(iota(tall[::-1], 1), iota(tall[::-1], 0))
    want_t[...] = wanted(iota(square, 0), iota(square, 1))
    want[...] = wanted(iota(square[::-1], 1), iota(square[::-1], 0))
    to_x[0].wait_recv()
    to_x[1].wait_recv()
    mixed = mixed_ref[...] + wide(x_in[...])
    mixed_ref[...] = mixed
    mean_sq = jnp.mean(mixed * mixed, axis=-1, keepdims=True)
    rounded = (mixed * lax.rsqrt(mean_sq + 1e-06) * gain[...]).astype(BF16)
    everything[z, y, x, c, :, :width] = rounded
    logits = lax.dot_general(rounded, router[...], over_last, preferred_element_type=F32)
    gates = jax.nn.sigmoid(logits)
    everything[z, y, x, c, :, width:] = jnp.concatenate([gates * hits, places], axis=1).astype(
        BF16
    )

    columns = [pl.ds(0, half), pl.ds(half, half + EXTRA)]
    first_peer, second_peer = [at.y_peer, at.x_peer], [at.x_peer, at.y_peer]

    def block(h, j, first_other, second_other):
        ys = first_other if h == 0 else second_other
        xs = second_other if h == 0 else first_other
        return everything.at[
            planes[j], 1 - y if ys else y, 1 - x if xs else x, c, :, columns[h]
        ]

    z_copies, first_copies, second_copies = {}, {}, {}
    core_copies = {j: [] for j in range(4)}
    sent = {j: [] for j in range(4)}

    def note(j, copy):
        sent[j].append(copy)
        return copy

    def core(j, spot):
        core_copies[j].append(note(j, send(spot, spot, at.core_peer)))

    def send_z(j):
        for h in (0, 1):
            spot = block(h, 0, 0, 0)
            z_copies[h, j] = note(0, send(spot, spot, at.z_peers[j]))

    def spread(j):
        for h in (0, 1):
            if j:
                z_copies[h, j].wait_recv()
            spot = block(h, j, 0, 0)
            first_copies[h, j] = note(j, send(spot, spot, first_peer[h]))
        for h in (0, 1):
            spot = block(h, j, 0, 0)
            second_copies[h, j, 0] = note(j, send(spot, spot, second_peer[h]))
        for h in (0, 1):
            core(j, block(h, j, 0, 0))

    def spread_first(j):
        for h in (0, 1):
            first_copies[h, j].wait_recv()
            spot = block(h, j, 1, 0)
            second_copies[h, j, 1] = note(j, send(spot, spot, second_peer[h]))
        for h in (0, 1):
            core(j, block(h, j, 1, 0))

    def spread_second(j):
        for other in (0, 1):
            for h in (0, 1):
                second_copies[h, j, other].wait_recv()
                core(j, block(h, j, other, 1))

    def dispatch(j):
        for copy in core_copies[j]:
            copy.wait_recv()

        def one_chip(i, carry):
            spot = everything.at[planes[j], i // 2, i % 2]
            tail = spot[:, :, width:].reshape(2 * rows, EXTRA)
            seats = lax.dot_general(pick_t[span:], tail, over_last, preferred_element_type=F32)
            table = jnp.where(seats == want_t[...], 1.0, 0.0).astype(BF16)
            local = jnp.dot(tail, pick[...], preferred_element_type=F32)
            combine[j, i] = jnp.where(local[:, span:] == want[...], local[:, :span], 0.0)
            packed = jnp.dot(
                table,
                spot[:, :, :width].reshape(2 * rows, width),
                preferred_element_type=F32,
            ).astype(BF16)
            for e in range(experts):
                slots[e, PLACE[j], pl.ds(pl.multiple_of(i * lanes, lanes), lanes), :] = packed[
                    e * lanes : (e + 1) * lanes
                ]
            return carry

        lax.fori_loop(0, 4, one_chip, 0)

    def feed(first_place, count_planes, first, last):
        here = pl.ds(first_place, count_planes)
        seats = slots.shape[2]

        def one_expert(e, carry):
            taken = slots[e, here].reshape(count_planes * seats, width)
            both = jnp.dot(taken, paired[e], preferred_element_type=F32)
            gate, up = both[:, :units], both[:, units:]
            hidden = (gate / (1.0 + jnp.exp(-gate)) * up).astype(BF16)
            for start in range(0, width, 512):
                out = jnp.dot(
                    hidden, down[e, :, start : start + 512], preferred_element_type=F32
                ).astype(BF16)
                slots[e, here, :, start : start + 512] = out.reshape(count_planes, seats, 512)
            return carry

        for e in range(first, last):
            one_expert(e, 0)

    peer_copies, first_sums, second_sums, z_sums = {}, {}, {}, {}
    orders = ((1, 1), (0, 1), (1, 0), (0, 0))

    def owner(j, fy, fx, core_id, h=None):
        cut = pl.ds(0, width) if h is None else halves[h]
        return (planes[j], 1 - y if fy else y, 1 - x if fx else x, core_id, slice(None), cut)

    def gather_sums(j):
        for copy in sent[j]:
            copy.wait_send()

        for turn, (fy, fx) in enumerate(orders):
            ys, xs = 1 - y if fy else y, 1 - x if fx else x
            i = ys * 2 + xs
            spot = pl.ds(pl.multiple_of(i * lanes, lanes), lanes)

            def piece(k, carry):
                cut = pl.ds(pl.multiple_of(k * 512, 512), 512)
                outs = jnp.concatenate(
                    [slots[e, PLACE[j], spot, cut] for e in range(experts)], axis=0
                )
                part = jnp.dot(combine[j, i].astype(BF16), outs, preferred_element_type=F32)
                for core_id in (0, 1):
                    everything[planes[j], ys, xs, core_id, :, cut] = part[
                        core_id * rows : (core_id + 1) * rows
                    ].astype(BF16)
                return carry

            lax.fori_loop(0, width // 512, piece, 0, unroll=True)
            peer_copies[j, fy, fx] = send(
                everything.at[owner(j, fy, fx, 1 - c)], peer_in.at[j, fy, fx], at.core_peer
            )
            if turn >= LAG:
                pass_first(j, *orders[turn - LAG])

    def both_cores(j, fy, fx, h):
        return wide(everything[owner(j, fy, fx, c, h)]) + wide(peer_in[j, fy, fx, :, halves[h]])

    def pass_first(j, fy, fx):
        peer_copies[j, fy, fx].wait_recv()
        for h in (0, 1):
            across, second = ((fx, fy), (fy, fx))[h]
            if across:
                first_out[j, h, second] = both_cores(j, fy, fx, h).astype(BF16)
                first_sums[j, h, second] = send(
                    first_out.at[j, h, second],
                    first_in.at[j, h, second],
                    (at.x_peer, at.y_peer)[h],
                )

    def sum_first(j):
        for fy, fx in orders[4 - LAG : 3]:
            pass_first(j, fy, fx)

    def sum_second(j):
        for h in (0, 1):
            first_sums[j, h, 1].wait_recv()
            fy, fx = (1, 0) if h == 0 else (0, 1)
            second_out[j, h] = (both_cores(j, fy, fx, h) + wide(first_in[j, h, 1])).astype(BF16)
            second_sums[j, h] = send(
                second_out.at[j, h], second_in.at[j, h], (at.y_peer, at.x_peer)[h]
            )

    def sum_plane(j):
        peer_copies[j, 0, 0].wait_recv()
        for h in (0, 1):
            first_sums[j, h, 0].wait_recv()
            second_sums[j, h].wait_recv()
            total = both_cores(j, 0, 0, h) + wide(first_in[j, h, 0]) + wide(second_in[j, h])
            if j:
                z_out[j - 1, h] = total.astype(BF16)
                z_sums[j, h] = send(z_out.at[j - 1, h], z_in.at[j - 1, h], at.z_peers[j])
            else:
                mixed_ref[:, halves[h]] = mixed_ref[:, halves[h]] + total

    def pages_out():
        for copy in page_y:
            copy.wait_recv()
        me = at.group.astype(F32)
        for slot in range(2):
            found = jnp.zeros(arrived_ref.shape[1:], F32)
            for zs in range(4):
                for ys in (0, 1):
                    held = wide(pages_in[zs, ys, slot])
                    found = found + jnp.where(held[16:17] == me, held[:16], 0.0)
            arrived_ref[slot] = found.astype(BF16)

    def finish():
        for h in (0, 1):
            value = mixed_ref[:, halves[h]]
            for j in Z_ORDER:
                z_sums[j, h].wait_recv()
                value = value + wide(z_in[j - 1, h])
            combined_ref[:, halves[h]] = value

    steps = dict(
        z=send_z, spread=spread, first=spread_first, second=spread_second, dispatch=dispatch,
        split=split_pairs, feed=feed, down=loads["down"].wait, sums=gather_sums, one=sum_first,
        two=sum_second, plane=sum_plane, pages=pages_out, finish=finish, page=pass_page,
    )
    for name, *given in SCHEDULE:
        steps[name](*given)
    waited = {id(copy) for j in range(4) for copy in sent[j]}
    for copy in used:
        if id(copy) not in waited:
            copy.wait_send()


PLACE = (0, 2, 1, 3)
Z_ORDER = (2, 3, 1)
LAG = 4
WARM = (("split", 0), ("split", 1), ("page", 1), ("split", 2), ("page", 2), ("page", 3), ("split", 3))
SCHEDULE = (
    ("z", 2), ("spread", 0), ("z", 1), ("first", 0), ("split", 4), ("spread", 2), ("z", 3),
    ("split", 5), ("second", 0), ("first", 2), ("split", 6), ("split", 7), ("spread", 1),
    ("dispatch", 0), ("second", 2), ("first", 1), ("dispatch", 2), ("down",), ("spread", 3),
    ("feed", 0, 2, 0, 4), ("second", 1), ("feed", 0, 2, 4, 8), ("first", 3), ("second", 3),
    ("sums", 2), ("dispatch", 1), ("one", 2), ("sums", 0), ("dispatch", 3), ("one", 0),
    ("feed", 2, 2, 0, 2), ("two", 2), ("feed", 2, 2, 2, 4), ("two", 0), ("plane", 2),
    ("feed", 2, 2, 4, 8), ("pages",), ("sums", 3), ("sums", 1), ("one", 3), ("one", 1),
    ("two", 3), ("plane", 3), ("two", 1), ("plane", 1), ("plane", 0), ("finish",),
)
COPIES = 3 + 4 + 6 + 2 * (3 + 4 + 8 + 16) + 16 + 16 + 8 + 6


def close_kernel(
    combined_hbm, gain_hbm, arrived_hbm, new_hbm, normed_hbm, out_hbm,
    combined, gain, new, normed, pages, sems,
):
    copies = [
        pltpu.make_async_copy(source, target, sems.at[index])
        for index, (source, target) in enumerate((
            (combined_hbm, combined), (gain_hbm, gain), (arrived_hbm, pages),
            (new, new_hbm), (normed, normed_hbm), (pages, out_hbm),
        ))
    ]
    for copy in copies[:3]:
        copy.start()
    copies[0].wait()
    value = combined[...]
    new[...] = value.astype(BF16)
    copies[3].start()
    copies[1].wait()
    scale = lax.rsqrt(jnp.mean(value * value, axis=-1, keepdims=True) + 1e-06)
    normed[...] = (value * scale * gain[...]).astype(BF16)
    copies[4].start()
    copies[2].wait()
    copies[5].start()
    for copy in copies[3:]:
        copy.wait()


def close(combined, gain, arrived):
    hbm = pl.BlockSpec(memory_space=pl.ANY)
    kept = jax.ShapeDtypeStruct(combined.shape, BF16)
    scratch = lambda value: pltpu.VMEM(value.shape, value.dtype)
    return pl.pallas_call(
        close_kernel,
        out_shape=(kept, kept, jax.ShapeDtypeStruct(arrived.shape, BF16)),
        in_specs=[hbm] * 3,
        out_specs=(hbm,) * 3,
        scratch_shapes=[scratch(v) for v in (combined, gain, kept, kept, arrived)]
        + [pltpu.SemaphoreType.DMA((6,))],
        name="close",
    )(combined, gain, arrived)


def whole_block(
    attn_out, out_weight, residual, norm_gain, router_weight, routes, gate_up, down_weight,
    final_gain, kv_pages, page_pick, destination,
):
    rows, width = residual.shape
    half = width // 2
    experts, _, _, units = gate_up.shape
    hbm, smem, vmem = (
        pl.BlockSpec(memory_space=space) for space in (pl.ANY, pltpu.SMEM, pltpu.VMEM)
    )
    scratch = lambda value: pltpu.VMEM(value.shape, value.dtype)
    blocks = lambda *shape: pltpu.VMEM(shape, BF16)
    page = kv_pages.shape[1:]
    gain = norm_gain.reshape(1, width)
    router, named = router_weight.T, routes.T
    combined, arrived = pl.pallas_call(
        block_kernel,
        out_shape=(
            jax.ShapeDtypeStruct((rows, width), F32),
            jax.ShapeDtypeStruct((2,) + page, BF16),
        ),
        in_specs=[smem] * 2 + [hbm] * 9,
        out_specs=(vmem,) * 2,
        scratch_shapes=[
            scratch(attn_out), scratch(out_weight), scratch(residual), scratch(gain),
            scratch(router), scratch(named),
            blocks(2, width, 2, units),
            blocks(experts, width, 2 * units),
            scratch(down_weight), scratch(kv_pages),
            blocks(4, rows, width),
            blocks(2, rows, width),
            blocks(rows, width),
            blocks(rows, width),
            pltpu.VMEM((rows, width), F32),
            blocks(4, 2, 2, 2, rows, width + EXTRA),
            blocks(experts, 4, 4 * 2 * CAP, width),
            pltpu.VMEM((4, 4, 2 * rows, experts * 2 * CAP), F32),
            blocks(2 * router_weight.shape[1], 2 * experts * 2 * CAP),
            blocks(2 * experts * 2 * CAP, 2 * router_weight.shape[1]),
            pltpu.VMEM((2 * rows, experts * 2 * CAP), F32),
            pltpu.VMEM((experts * 2 * CAP, 2 * rows), F32),
            blocks(4, 2, 2, rows, width),
            blocks(4, 2, 2, rows, half),
            blocks(4, 2, 2, rows, half),
            blocks(4, 2, rows, half),
            blocks(4, 2, rows, half),
            blocks(3, 2, rows, half),
            blocks(3, 2, rows, half),
            blocks(4, 2, 2, page[0] + 1, page[1], page[2]),
            pltpu.SemaphoreType.DMA((8,)),
            pltpu.SemaphoreType.DMA((2,)),
            pltpu.SemaphoreType.DMA((COPIES,)),
            pltpu.SemaphoreType.DMA((COPIES,)),
        ],
        compiler_params=pltpu.CompilerParams(
            collective_id=0, has_side_effects=True, vmem_limit_bytes=60 << 20
        ),
        name="block",
    )(
        page_pick, destination, attn_out, out_weight, residual, gain, router, named,
        gate_up, down_weight, kv_pages,
    )
    return close(combined, final_gain.reshape(1, width), arrived)


def pair_kernel(taken_ref, paired_ref, out_ref):
    units = paired_ref.shape[3]
    both = jnp.swapaxes(paired_ref[0], 0, 1)
    for part in (0, 1):
        out_ref[0, :, part * units : (part + 1) * units] = jnp.dot(
            taken_ref[0], both[part], preferred_element_type=F32
        )


def pair_products(taken, gate_up):
    experts, count, width = taken.shape
    units = gate_up.shape[3]
    step = 256 if count % 256 == 0 else count
    return pl.pallas_call(
        pair_kernel,
        grid=(experts, count // step),
        out_shape=jax.ShapeDtypeStruct((experts, count, 2 * units), F32),
        in_specs=[
            pl.BlockSpec((1, step, width), lambda e, i: (e, i, 0)),
            pl.BlockSpec((1, width, 2, units), lambda e, i: (e, 0, 0, 0)),
        ],
        out_specs=pl.BlockSpec((1, step, 2 * units), lambda e, i: (e, i, 0)),
        compiler_params=pltpu.CompilerParams(vmem_limit_bytes=32 << 20),
        name="pair",
    )(taken, gate_up)


def migrate(kv_pages, page_pick, destination):
    groups = lax.axis_size("dp")
    chosen_pages = jnp.concatenate(
        [
            lax.dynamic_slice_in_dim(kv_pages, page_pick[0, slot], 1, axis=0)
            for slot in range(page_pick.shape[1])
        ],
        axis=0,
    )
    owners = jnp.arange(groups, dtype=jnp.int32)[:, None] == destination[0][None, :]
    outgoing = jnp.where(
        owners[:, :, None, None, None], chosen_pages[None], jnp.zeros((), kv_pages.dtype)
    )
    incoming = lax.all_to_all(outgoing, "dp", split_axis=0, concat_axis=0, tiled=True)
    return jnp.sum(incoming, axis=0)


def local_slots(routes_all, first, local_experts, groups, shards, rows):
    hits = jnp.any(
        routes_all[:, :, None] == first + jnp.arange(local_experts, dtype=jnp.int32), axis=1
    )
    hits = hits.reshape(groups, shards * rows, local_experts)
    token = jnp.arange(shards * rows, dtype=jnp.int32)
    before = (token[:, None] > token[None, :]) & (
        token[:, None] // rows == token[None, :] // rows
    )
    rank = jnp.einsum(
        "ut,bte->bue",
        before.astype(jnp.bfloat16),
        hits.astype(jnp.bfloat16),
        preferred_element_type=jnp.float32,
    ).astype(jnp.int32)
    within = (token // rows * CAP)[None, :, None] + rank
    within = jnp.where(hits, within, -1)
    slots = jnp.arange(shards * CAP, dtype=jnp.int32)
    table = within[:, :, :, None] == slots
    return table.reshape(groups, shards * rows, local_experts * shards * CAP)


def per_device(
    attn_out,
    residual,
    out_weight,
    norm_gain,
    router_weight,
    routes,
    gate_up,
    down_weight,
    final_gain,
    kv_pages,
    page_pick,
    destination,
):
    groups = lax.axis_size("dp")
    shards = lax.axis_size("tensor")
    rows, width = residual.shape
    local_experts = gate_up.shape[0]
    first = lax.axis_index("dp") * local_experts
    if groups == 8 and shards == 4:
        return whole_block(
            attn_out, out_weight, residual, norm_gain, router_weight, routes, gate_up,
            down_weight, final_gain, kv_pages, page_pick, destination,
        )
    arrived = migrate(kv_pages, page_pick, destination)
    routes_all = lax.all_gather(routes, ("dp", "tensor"), axis=0, tiled=True)
    projected = lax.psum_scatter(
        jnp.dot(attn_out, out_weight, preferred_element_type=jnp.float32).astype(
            jnp.bfloat16
        ),
        "tensor",
        scatter_dimension=0,
        tiled=True,
    ).astype(jnp.float32)
    mixed_sum = residual.astype(jnp.float32) + projected
    normed_in = rms_scale(mixed_sum, norm_gain).astype(jnp.bfloat16)
    tokens = lax.all_gather(normed_in, ("dp", "tensor"), axis=0, tiled=True)
    table = local_slots(routes_all, first, local_experts, groups, shards, rows)
    local_router = lax.dynamic_slice_in_dim(router_weight, first, local_experts, axis=1)
    logits = jnp.dot(tokens, local_router, preferred_element_type=jnp.float32)
    gates = jax.nn.sigmoid(logits).astype(jnp.bfloat16)
    tokens = tokens.reshape(groups, shards * rows, width)
    gates = jnp.repeat(
        gates.reshape(groups, shards * rows, local_experts), shards * CAP, axis=2
    )
    placement = table.astype(jnp.bfloat16)
    combine = jnp.where(table, gates, jnp.zeros((), jnp.bfloat16))
    slotted = jnp.einsum(
        "bts,btd->bsd", placement, tokens, preferred_element_type=jnp.float32
    ).astype(jnp.bfloat16)
    slotted = slotted.reshape(groups, local_experts, shards * CAP, width)
    units = gate_up.shape[3]
    taken = jnp.swapaxes(slotted, 0, 1).reshape(local_experts, -1, width)
    paired = pair_products(taken, gate_up)
    paired = jnp.swapaxes(paired.reshape(local_experts, groups, shards * CAP, 2 * units), 0, 1)
    hidden = (jax.nn.silu(paired[..., :units]) * paired[..., units:]).astype(jnp.bfloat16)
    expert_out = jnp.einsum(
        "becf,efd->becd", hidden, down_weight, preferred_element_type=jnp.float32
    ).astype(jnp.bfloat16)
    expert_out = expert_out.reshape(groups, local_experts * shards * CAP, width)
    partial = jnp.einsum(
        "bts,bsd->btd", combine, expert_out, preferred_element_type=jnp.float32
    ).astype(jnp.bfloat16)
    moe_sum = lax.psum_scatter(
        partial.reshape(groups * shards * rows, width),
        ("dp", "tensor"),
        scatter_dimension=0,
        tiled=True,
    ).astype(jnp.float32)
    combined = mixed_sum + moe_sum
    new_residual = combined.astype(jnp.bfloat16)
    normed = rms_scale(combined, final_gain).astype(jnp.bfloat16)
    return (new_residual, normed, arrived)


def solution(mesh):
    in_specs = (
        P("dp", "tensor"),
        P(("dp", "tensor"), None),
        P("tensor", None),
        P(),
        P(),
        P(("dp", "tensor"), None),
        P("dp", None, None, "tensor"),
        P("dp", "tensor", None),
        P(),
        P("dp", None, "tensor", None),
        P("dp", None),
        P("dp", None),
    )
    out_specs = (
        P(("dp", "tensor"), None),
        P(("dp", "tensor"), None),
        P("dp", None, "tensor", None),
    )
    return jax.shard_map(
        per_device, mesh=mesh, in_specs=in_specs, out_specs=out_specs, check_vma=False
    )
```

```python
import jax
import jax.numpy as jnp
from jax import lax
from jax.experimental import pallas as pl
from jax.experimental.pallas import tpu as pltpu
from jax.sharding import PartitionSpec as P

CAP = 8


def rms_scale(values, gain_vec):
    mean_sq = jnp.mean(values * values, axis=-1, keepdims=True)
    return values * lax.rsqrt(mean_sq + 1e-06) * gain_vec


MESH = pl.DeviceIdType.MESH
EXTRA = 128
F32, BF16 = jnp.float32, jnp.bfloat16


def wide(value):
    return value.astype(F32)


class Place:
    def __init__(self):
        group, shard = lax.axis_index("dp"), lax.axis_index("tensor")
        z, y, x, c = group // 2, group % 2, shard // 2, shard % 2
        self.group, self.z, self.y, self.x, self.c = group, z, y, x, c
        self.planes = [z, z + 1 - 2 * (z % 2), (z + 2) % 4, 3 - z]
        self.core_peer = (group, x * 2 + 1 - c)
        self.x_peer = (group, (1 - x) * 2 + c)
        self.y_peer = (z * 2 + 1 - y, shard)
        self.z_peers = [None] + [(plane * 2 + y, shard) for plane in self.planes[1:]]

    def enter(self):
        barrier = pltpu.get_barrier_semaphore()
        peers = [self.core_peer, self.x_peer, self.y_peer] + self.z_peers[1:]
        for peer in peers:
            pl.semaphore_signal(barrier, inc=1, device_id=peer, device_id_type=MESH)
        pl.semaphore_wait(barrier, len(peers))


def sender(send_sems, recv_sems):
    used = []

    def send(source, target, peer):
        index = len(used)
        copy = pltpu.make_async_remote_copy(
            src_ref=source,
            dst_ref=target,
            send_sem=send_sems.at[index],
            recv_sem=recv_sems.at[index],
            device_id=peer,
            device_id_type=MESH,
        )
        copy.start()
        used.append(copy)
        return copy

    return send, used


def block_kernel(
    pick_ref, target_ref,
    attn_hbm, weight_hbm, residual_hbm, gain_hbm, router_hbm, routes_hbm,
    paired_hbm, down_hbm, kv_hbm,
    combined_ref, arrived_ref,
    attn, weight, residual, gain, router, routes, staged, paired, down, kv,
    made, core_in, x_out, x_in, mixed_ref, everything, slots, combine,
    pick, pick_t, want, want_t, peer_in, first_out, first_in, second_out, second_in, z_out, z_in, pages_in,
    local_sems, stage_sems, send_sems, recv_sems,
):
    at = Place()
    z, y, x, c, planes = at.z, at.y, at.x, at.c, at.planes
    rows, width = residual.shape
    half = width // 2
    experts = paired.shape[0]
    units = down.shape[1]
    loads = {}
    for index, (name, source, target) in enumerate((
        ("attn", attn_hbm, attn), ("weight", weight_hbm, weight), ("kv", kv_hbm, kv),
        ("residual", residual_hbm, residual), ("gain", gain_hbm, gain),
        ("router", router_hbm, router), ("routes", routes_hbm, routes),
        ("down", down_hbm, down),
    )):
        loads[name] = pltpu.make_async_copy(source, target, local_sems.at[index])

    def stage(e):
        return pltpu.make_async_copy(paired_hbm.at[e], staged.at[e % 2], stage_sems.at[e % 2])

    for name in ("attn", "weight", "kv", "residual", "gain", "router", "routes"):
        loads[name].start()
    stage(0).start()
    stage(1).start()
    loads["down"].start()

    def split_pairs(e):
        stage(e).wait()

        def piece(i, carry):
            spot = pl.ds(pl.multiple_of(i * 128, 128), 128)
            both = jnp.swapaxes(staged[e % 2, spot], 0, 1)
            paired[e, spot, :units] = both[0]
            paired[e, spot, units:] = both[1]
            return carry

        lax.fori_loop(0, width // 128, piece, 0)
        if e + 2 < experts:
            stage(e + 2).start()

    at.enter()
    send, used = sender(send_sems, recv_sems)

    loads["kv"].wait()
    for slot in range(2):
        pages_in[z, y, slot, pl.ds(0, 16)] = kv[pick_ref[0, slot]]
        pages_in[z, y, slot, 16] = jnp.full(kv.shape[2:], target_ref[0, slot], jnp.int32).astype(
            F32
        ).astype(BF16)
    own_pages = pages_in.at[z, y]
    page_z = [None] + [send(own_pages, own_pages, at.z_peers[j]) for j in (1, 2, 3)]
    page_y = [send(own_pages, own_pages, at.y_peer)]

    def pass_page(j):
        page_z[j].wait_recv()
        spot = pages_in.at[planes[j], y]
        page_y.append(send(spot, spot, at.y_peer))

    loads["attn"].wait()
    loads["weight"].wait()
    halves = [pl.ds(0, half), pl.ds(half, half)]
    far, near, to_x = [], [], []
    for h in (0, 1):
        for start in range(h * half, h * half + half, 512):
            part = jnp.dot(
                attn[...], weight[:, start : start + 512], preferred_element_type=F32
            )
            for shard in range(4):
                made[shard, :, start : start + 512] = part[
                    shard * rows : (shard + 1) * rows
                ].astype(BF16)
        far.append(
            send(made.at[(1 - x) * 2 + 1 - c, :, halves[h]], core_in.at[0, :, halves[h]], at.core_peer)
        )
    for h in (0, 1):
        near.append(
            send(made.at[x * 2 + 1 - c, :, halves[h]], core_in.at[1, :, halves[h]], at.core_peer)
        )
    for h in (0, 1):
        far[h].wait_recv()
        x_out[:, halves[h]] = (
            wide(made[(1 - x) * 2 + c, :, halves[h]]) + wide(core_in[0, :, halves[h]])
        ).astype(BF16)
        to_x.append(send(x_out.at[:, halves[h]], x_in.at[:, halves[h]], at.x_peer))
    for name, index in WARM:
        {"split": split_pairs, "page": pass_page}[name](index)
    loads["residual"].wait()
    for h in (0, 1):
        near[h].wait_recv()
        mixed_ref[:, halves[h]] = (
            wide(residual[:, halves[h]])
            + wide(made[x * 2 + c, :, halves[h]])
            + wide(core_in[1, :, halves[h]])
        )
    loads["gain"].wait()
    loads["router"].wait()
    loads["routes"].wait()
    count = router.shape[0]
    named = routes[...]
    expert = lax.broadcasted_iota(jnp.int32, (count, rows), 0)
    hits_t = jnp.zeros((count, rows), F32)
    for k in range(named.shape[0]):
        hits_t = hits_t + jnp.where(named[k : k + 1, :] == expert, 1.0, 0.0)
    later = lax.broadcasted_iota(jnp.int32, (rows, rows), 0)
    sooner = lax.broadcasted_iota(jnp.int32, (rows, rows), 1)
    eye = jnp.where(later == sooner, 1.0, 0.0).astype(BF16)
    over_last = (((1,), (1,)), ((), ()))
    hits = lax.dot_general(eye, hits_t.astype(BF16), over_last, preferred_element_type=F32)
    before = jnp.where(later > sooner, 1.0, 0.0).astype(BF16)
    places = hits * (1.0 + jnp.dot(before, hits.astype(BF16), preferred_element_type=F32))
    lanes = 2 * CAP
    span = experts * lanes
    first_expert = at.group * experts

    def iota(shape, axis):
        return lax.broadcasted_iota(jnp.int32, shape, axis)

    def wanted(slot, token):
        return wide(jnp.where(slot // CAP % 2 == token // rows, slot % CAP + 1, -1))

    def picks(slot, entry):
        chosen = first_expert + slot % span // lanes + slot // span * count
        return jnp.where(chosen == entry, 1.0, 0.0).astype(BF16)

    tall, square = (2 * span, 2 * count), (span, 2 * rows)
    pick_t[...] = picks(iota(tall, 0), iota(tall, 1))
    pick[...] = picks(iota(tall[::-1], 1), iota(tall[::-1], 0))
    want_t[...] = wanted(iota(square, 0), iota(square, 1))
    want[...] = wanted(iota(square[::-1], 1), iota(square[::-1], 0))
    to_x[0].wait_recv()
    to_x[1].wait_recv()
    mixed = mixed_ref[...] + wide(x_in[...])
    mixed_ref[...] = mixed
    mean_sq = jnp.mean(mixed * mixed, axis=-1, keepdims=True)
    rounded = (mixed * lax.rsqrt(mean_sq + 1e-06) * gain[...]).astype(BF16)
    everything[z, y, x, c, :, :width] = rounded
    logits = lax.dot_general(rounded, router[...], over_last, preferred_element_type=F32)
    gates = jax.nn.sigmoid(logits)
    everything[z, y, x, c, :, width:] = jnp.concatenate([gates * hits, places], axis=1).astype(
        BF16
    )

    columns = [pl.ds(0, half), pl.ds(half, half + EXTRA)]
    first_peer, second_peer = [at.y_peer, at.x_peer], [at.x_peer, at.y_peer]

    def block(h, j, first_other, second_other):
        ys = first_other if h == 0 else second_other
        xs = second_other if h == 0 else first_other
        return everything.at[
            planes[j], 1 - y if ys else y, 1 - x if xs else x, c, :, columns[h]
        ]

    z_copies, first_copies, second_copies = {}, {}, {}
    core_copies = {j: [] for j in range(4)}
    sent = {j: [] for j in range(4)}

    def note(j, copy):
        sent[j].append(copy)
        return copy

    def core(j, spot):
        core_copies[j].append(note(j, send(spot, spot, at.core_peer)))

    def send_z(j):
        for h in (0, 1):
            spot = block(h, 0, 0, 0)
            z_copies[h, j] = note(0, send(spot, spot, at.z_peers[j]))

    def spread(j):
        for h in (0, 1):
            if j:
                z_copies[h, j].wait_recv()
            spot = block(h, j, 0, 0)
            first_copies[h, j] = note(j, send(spot, spot, first_peer[h]))
        for h in (0, 1):
            spot = block(h, j, 0, 0)
            second_copies[h, j, 0] = note(j, send(spot, spot, second_peer[h]))
        for h in (0, 1):
            core(j, block(h, j, 0, 0))

    def spread_first(j):
        for h in (0, 1):
            first_copies[h, j].wait_recv()
            spot = block(h, j, 1, 0)
            second_copies[h, j, 1] = note(j, send(spot, spot, second_peer[h]))
        for h in (0, 1):
            core(j, block(h, j, 1, 0))

    def spread_second(j):
        for other in (0, 1):
            for h in (0, 1):
                second_copies[h, j, other].wait_recv()
                core(j, block(h, j, other, 1))

    def dispatch(j):
        for copy in core_copies[j]:
            copy.wait_recv()

        def one_chip(i, carry):
            spot = everything.at[planes[j], i // 2, i % 2]
            tail = spot[:, :, width:].reshape(2 * rows, EXTRA)
            seats = lax.dot_general(pick_t[span:], tail, over_last, preferred_element_type=F32)
            table = jnp.where(seats == want_t[...], 1.0, 0.0).astype(BF16)
            local = jnp.dot(tail, pick[...], preferred_element_type=F32)
            combine[j, i] = jnp.where(local[:, span:] == want[...], local[:, :span], 0.0)
            packed = jnp.dot(
                table,
                spot[:, :, :width].reshape(2 * rows, width),
                preferred_element_type=F32,
            ).astype(BF16)
            for e in range(experts):
                slots[e, PLACE[j], pl.ds(pl.multiple_of(i * lanes, lanes), lanes), :] = packed[
                    e * lanes : (e + 1) * lanes
                ]
            return carry

        lax.fori_loop(0, 4, one_chip, 0)

    def feed(first_place, count_planes, first, last):
        here = pl.ds(first_place, count_planes)
        seats = slots.shape[2]

        def one_expert(e, carry):
            taken = slots[e, here].reshape(count_planes * seats, width)
            both = jnp.dot(taken, paired[e], preferred_element_type=F32)
            gate, up = both[:, :units], both[:, units:]
            hidden = (gate / (1.0 + jnp.exp(-gate)) * up).astype(BF16)
            for start in range(0, width, 512):
                out = jnp.dot(
                    hidden, down[e, :, start : start + 512], preferred_element_type=F32
                ).astype(BF16)
                slots[e, here, :, start : start + 512] = out.reshape(count_planes, seats, 512)
            return carry

        for e in range(first, last):
            one_expert(e, 0)

    peer_copies, first_sums, second_sums, z_sums = {}, {}, {}, {}
    orders = ((1, 1), (0, 1), (1, 0), (0, 0))

    def owner(j, fy, fx, core_id, h=None):
        cut = pl.ds(0, width) if h is None else halves[h]
        return (planes[j], 1 - y if fy else y, 1 - x if fx else x, core_id, slice(None), cut)

    def gather_sums(j):
        for copy in sent[j]:
            copy.wait_send()

        for turn, (fy, fx) in enumerate(orders):
            ys, xs = 1 - y if fy else y, 1 - x if fx else x
            i = ys * 2 + xs
            spot = pl.ds(pl.multiple_of(i * lanes, lanes), lanes)

            def piece(k, carry):
                cut = pl.ds(pl.multiple_of(k * 512, 512), 512)
                outs = jnp.concatenate(
                    [slots[e, PLACE[j], spot, cut] for e in range(experts)], axis=0
                )
                part = jnp.dot(combine[j, i].astype(BF16), outs, preferred_element_type=F32)
                for core_id in (0, 1):
                    everything[planes[j], ys, xs, core_id, :, cut] = part[
                        core_id * rows : (core_id + 1) * rows
                    ].astype(BF16)
                return carry

            lax.fori_loop(0, width // 512, piece, 0, unroll=True)
            peer_copies[j, fy, fx] = send(
                everything.at[owner(j, fy, fx, 1 - c)], peer_in.at[j, fy, fx], at.core_peer
            )
            if turn >= LAG:
                pass_first(j, *orders[turn - LAG])

    def both_cores(j, fy, fx, h):
        return wide(everything[owner(j, fy, fx, c, h)]) + wide(peer_in[j, fy, fx, :, halves[h]])

    def pass_first(j, fy, fx):
        peer_copies[j, fy, fx].wait_recv()
        for h in (0, 1):
            across, second = ((fx, fy), (fy, fx))[h]
            if across:
                first_out[j, h, second] = both_cores(j, fy, fx, h).astype(BF16)
                first_sums[j, h, second] = send(
                    first_out.at[j, h, second],
                    first_in.at[j, h, second],
                    (at.x_peer, at.y_peer)[h],
                )

    def sum_first(j):
        for fy, fx in orders[4 - LAG : 3]:
            pass_first(j, fy, fx)

    def sum_second(j):
        for h in (0, 1):
            first_sums[j, h, 1].wait_recv()
            fy, fx = (1, 0) if h == 0 else (0, 1)
            second_out[j, h] = (both_cores(j, fy, fx, h) + wide(first_in[j, h, 1])).astype(BF16)
            second_sums[j, h] = send(
                second_out.at[j, h], second_in.at[j, h], (at.y_peer, at.x_peer)[h]
            )

    def sum_plane(j):
        peer_copies[j, 0, 0].wait_recv()
        for h in (0, 1):
            first_sums[j, h, 0].wait_recv()
            second_sums[j, h].wait_recv()
            total = both_cores(j, 0, 0, h) + wide(first_in[j, h, 0]) + wide(second_in[j, h])
            if j:
                z_out[j - 1, h] = total.astype(BF16)
                z_sums[j, h] = send(z_out.at[j - 1, h], z_in.at[j - 1, h], at.z_peers[j])
            else:
                mixed_ref[:, halves[h]] = mixed_ref[:, halves[h]] + total

    def pages_out():
        for copy in page_y:
            copy.wait_recv()
        me = at.group.astype(F32)
        for slot in range(2):
            found = jnp.zeros(arrived_ref.shape[1:], F32)
            for zs in range(4):
                for ys in (0, 1):
                    held = wide(pages_in[zs, ys, slot])
                    found = found + jnp.where(held[16:17] == me, held[:16], 0.0)
            arrived_ref[slot] = found.astype(BF16)

    def finish():
        for h in (0, 1):
            value = mixed_ref[:, halves[h]]
            for j in Z_ORDER:
                z_sums[j, h].wait_recv()
                value = value + wide(z_in[j - 1, h])
            combined_ref[:, halves[h]] = value

    steps = dict(
        z=send_z, spread=spread, first=spread_first, second=spread_second, dispatch=dispatch,
        split=split_pairs, feed=feed, down=loads["down"].wait, sums=gather_sums, one=sum_first,
        two=sum_second, plane=sum_plane, pages=pages_out, finish=finish, page=pass_page,
    )
    for name, *given in SCHEDULE:
        steps[name](*given)
    waited = {id(copy) for j in range(4) for copy in sent[j]}
    for copy in used:
        if id(copy) not in waited:
            copy.wait_send()


PLACE = (0, 2, 1, 3)
Z_ORDER = (2, 3, 1)
LAG = 4
WARM = (("split", 0), ("split", 1), ("page", 1), ("split", 2), ("page", 2), ("page", 3), ("split", 3))
SCHEDULE = (
    ("z", 2), ("spread", 0), ("z", 1), ("first", 0), ("split", 4), ("spread", 2), ("z", 3),
    ("split", 5), ("second", 0), ("first", 2), ("split", 6), ("split", 7), ("spread", 1),
    ("dispatch", 0), ("second", 2), ("first", 1), ("dispatch", 2), ("down",), ("spread", 3),
    ("feed", 0, 2, 0, 4), ("second", 1), ("feed", 0, 2, 4, 8), ("first", 3), ("second", 3),
    ("sums", 2), ("dispatch", 1), ("one", 2), ("sums", 0), ("dispatch", 3), ("one", 0),
    ("feed", 2, 2, 0, 4), ("two", 2), ("two", 0), ("feed", 2, 2, 4, 8), ("pages",), ("sums", 3),
    ("plane", 2), ("sums", 1), ("one", 3), ("two", 3), ("one", 1), ("plane", 3), ("two", 1),
    ("plane", 1), ("plane", 0), ("finish",),
)
COPIES = 3 + 4 + 6 + 2 * (3 + 4 + 8 + 16) + 16 + 16 + 8 + 6


def close_kernel(
    combined_hbm, gain_hbm, arrived_hbm, new_hbm, normed_hbm, out_hbm,
    combined, gain, new, normed, pages, sems,
):
    copies = [
        pltpu.make_async_copy(source, target, sems.at[index])
        for index, (source, target) in enumerate((
            (combined_hbm, combined), (gain_hbm, gain), (arrived_hbm, pages),
            (new, new_hbm), (normed, normed_hbm), (pages, out_hbm),
        ))
    ]
    for copy in copies[:3]:
        copy.start()
    copies[0].wait()
    value = combined[...]
    new[...] = value.astype(BF16)
    copies[3].start()
    copies[1].wait()
    scale = lax.rsqrt(jnp.mean(value * value, axis=-1, keepdims=True) + 1e-06)
    normed[...] = (value * scale * gain[...]).astype(BF16)
    copies[4].start()
    copies[2].wait()
    copies[5].start()
    for copy in copies[3:]:
        copy.wait()


def close(combined, gain, arrived):
    hbm = pl.BlockSpec(memory_space=pl.ANY)
    kept = jax.ShapeDtypeStruct(combined.shape, BF16)
    scratch = lambda value: pltpu.VMEM(value.shape, value.dtype)
    return pl.pallas_call(
        close_kernel,
        out_shape=(kept, kept, jax.ShapeDtypeStruct(arrived.shape, BF16)),
        in_specs=[hbm] * 3,
        out_specs=(hbm,) * 3,
        scratch_shapes=[scratch(v) for v in (combined, gain, kept, kept, arrived)]
        + [pltpu.SemaphoreType.DMA((6,))],
        name="close",
    )(combined, gain, arrived)


def whole_block(
    attn_out, out_weight, residual, norm_gain, router_weight, routes, gate_up, down_weight,
    final_gain, kv_pages, page_pick, destination,
):
    rows, width = residual.shape
    half = width // 2
    experts, _, _, units = gate_up.shape
    hbm, smem, vmem = (
        pl.BlockSpec(memory_space=space) for space in (pl.ANY, pltpu.SMEM, pltpu.VMEM)
    )
    scratch = lambda value: pltpu.VMEM(value.shape, value.dtype)
    blocks = lambda *shape: pltpu.VMEM(shape, BF16)
    page = kv_pages.shape[1:]
    gain = norm_gain.reshape(1, width)
    router, named = router_weight.T, routes.T
    combined, arrived = pl.pallas_call(
        block_kernel,
        out_shape=(
            jax.ShapeDtypeStruct((rows, width), F32),
            jax.ShapeDtypeStruct((2,) + page, BF16),
        ),
        in_specs=[smem] * 2 + [hbm] * 9,
        out_specs=(vmem,) * 2,
        scratch_shapes=[
            scratch(attn_out), scratch(out_weight), scratch(residual), scratch(gain),
            scratch(router), scratch(named),
            blocks(2, width, 2, units),
            blocks(experts, width, 2 * units),
            scratch(down_weight), scratch(kv_pages),
            blocks(4, rows, width),
            blocks(2, rows, width),
            blocks(rows, width),
            blocks(rows, width),
            pltpu.VMEM((rows, width), F32),
            blocks(4, 2, 2, 2, rows, width + EXTRA),
            blocks(experts, 4, 4 * 2 * CAP, width),
            pltpu.VMEM((4, 4, 2 * rows, experts * 2 * CAP), F32),
            blocks(2 * router_weight.shape[1], 2 * experts * 2 * CAP),
            blocks(2 * experts * 2 * CAP, 2 * router_weight.shape[1]),
            pltpu.VMEM((2 * rows, experts * 2 * CAP), F32),
            pltpu.VMEM((experts * 2 * CAP, 2 * rows), F32),
            blocks(4, 2, 2, rows, width),
            blocks(4, 2, 2, rows, half),
            blocks(4, 2, 2, rows, half),
            blocks(4, 2, rows, half),
            blocks(4, 2, rows, half),
            blocks(3, 2, rows, half),
            blocks(3, 2, rows, half),
            blocks(4, 2, 2, page[0] + 1, page[1], page[2]),
            pltpu.SemaphoreType.DMA((8,)),
            pltpu.SemaphoreType.DMA((2,)),
            pltpu.SemaphoreType.DMA((COPIES,)),
            pltpu.SemaphoreType.DMA((COPIES,)),
        ],
        compiler_params=pltpu.CompilerParams(
            collective_id=0, has_side_effects=True, vmem_limit_bytes=60 << 20
        ),
        name="block",
    )(
        page_pick, destination, attn_out, out_weight, residual, gain, router, named,
        gate_up, down_weight, kv_pages,
    )
    return close(combined, final_gain.reshape(1, width), arrived)


def pair_kernel(taken_ref, paired_ref, out_ref):
    units = paired_ref.shape[3]
    both = jnp.swapaxes(paired_ref[0], 0, 1)
    for part in (0, 1):
        out_ref[0, :, part * units : (part + 1) * units] = jnp.dot(
            taken_ref[0], both[part], preferred_element_type=F32
        )


def pair_products(taken, gate_up):
    experts, count, width = taken.shape
    units = gate_up.shape[3]
    step = 256 if count % 256 == 0 else count
    return pl.pallas_call(
        pair_kernel,
        grid=(experts, count // step),
        out_shape=jax.ShapeDtypeStruct((experts, count, 2 * units), F32),
        in_specs=[
            pl.BlockSpec((1, step, width), lambda e, i: (e, i, 0)),
            pl.BlockSpec((1, width, 2, units), lambda e, i: (e, 0, 0, 0)),
        ],
        out_specs=pl.BlockSpec((1, step, 2 * units), lambda e, i: (e, i, 0)),
        compiler_params=pltpu.CompilerParams(vmem_limit_bytes=32 << 20),
        name="pair",
    )(taken, gate_up)


def migrate(kv_pages, page_pick, destination):
    groups = lax.axis_size("dp")
    chosen_pages = jnp.concatenate(
        [
            lax.dynamic_slice_in_dim(kv_pages, page_pick[0, slot], 1, axis=0)
            for slot in range(page_pick.shape[1])
        ],
        axis=0,
    )
    owners = jnp.arange(groups, dtype=jnp.int32)[:, None] == destination[0][None, :]
    outgoing = jnp.where(
        owners[:, :, None, None, None], chosen_pages[None], jnp.zeros((), kv_pages.dtype)
    )
    incoming = lax.all_to_all(outgoing, "dp", split_axis=0, concat_axis=0, tiled=True)
    return jnp.sum(incoming, axis=0)


def local_slots(routes_all, first, local_experts, groups, shards, rows):
    hits = jnp.any(
        routes_all[:, :, None] == first + jnp.arange(local_experts, dtype=jnp.int32), axis=1
    )
    hits = hits.reshape(groups, shards * rows, local_experts)
    token = jnp.arange(shards * rows, dtype=jnp.int32)
    before = (token[:, None] > token[None, :]) & (
        token[:, None] // rows == token[None, :] // rows
    )
    rank = jnp.einsum(
        "ut,bte->bue",
        before.astype(jnp.bfloat16),
        hits.astype(jnp.bfloat16),
        preferred_element_type=jnp.float32,
    ).astype(jnp.int32)
    within = (token // rows * CAP)[None, :, None] + rank
    within = jnp.where(hits, within, -1)
    slots = jnp.arange(shards * CAP, dtype=jnp.int32)
    table = within[:, :, :, None] == slots
    return table.reshape(groups, shards * rows, local_experts * shards * CAP)


def per_device(
    attn_out,
    residual,
    out_weight,
    norm_gain,
    router_weight,
    routes,
    gate_up,
    down_weight,
    final_gain,
    kv_pages,
    page_pick,
    destination,
):
    groups = lax.axis_size("dp")
    shards = lax.axis_size("tensor")
    rows, width = residual.shape
    local_experts = gate_up.shape[0]
    first = lax.axis_index("dp") * local_experts
    if groups == 8 and shards == 4:
        return whole_block(
            attn_out, out_weight, residual, norm_gain, router_weight, routes, gate_up,
            down_weight, final_gain, kv_pages, page_pick, destination,
        )
    arrived = migrate(kv_pages, page_pick, destination)
    routes_all = lax.all_gather(routes, ("dp", "tensor"), axis=0, tiled=True)
    projected = lax.psum_scatter(
        jnp.dot(attn_out, out_weight, preferred_element_type=jnp.float32).astype(
            jnp.bfloat16
        ),
        "tensor",
        scatter_dimension=0,
        tiled=True,
    ).astype(jnp.float32)
    mixed_sum = residual.astype(jnp.float32) + projected
    normed_in = rms_scale(mixed_sum, norm_gain).astype(jnp.bfloat16)
    tokens = lax.all_gather(normed_in, ("dp", "tensor"), axis=0, tiled=True)
    table = local_slots(routes_all, first, local_experts, groups, shards, rows)
    local_router = lax.dynamic_slice_in_dim(router_weight, first, local_experts, axis=1)
    logits = jnp.dot(tokens, local_router, preferred_element_type=jnp.float32)
    gates = jax.nn.sigmoid(logits).astype(jnp.bfloat16)
    tokens = tokens.reshape(groups, shards * rows, width)
    gates = jnp.repeat(
        gates.reshape(groups, shards * rows, local_experts), shards * CAP, axis=2
    )
    placement = table.astype(jnp.bfloat16)
    combine = jnp.where(table, gates, jnp.zeros((), jnp.bfloat16))
    slotted = jnp.einsum(
        "bts,btd->bsd", placement, tokens, preferred_element_type=jnp.float32
    ).astype(jnp.bfloat16)
    slotted = slotted.reshape(groups, local_experts, shards * CAP, width)
    units = gate_up.shape[3]
    taken = jnp.swapaxes(slotted, 0, 1).reshape(local_experts, -1, width)
    paired = pair_products(taken, gate_up)
    paired = jnp.swapaxes(paired.reshape(local_experts, groups, shards * CAP, 2 * units), 0, 1)
    hidden = (jax.nn.silu(paired[..., :units]) * paired[..., units:]).astype(jnp.bfloat16)
    expert_out = jnp.einsum(
        "becf,efd->becd", hidden, down_weight, preferred_element_type=jnp.float32
    ).astype(jnp.bfloat16)
    expert_out = expert_out.reshape(groups, local_experts * shards * CAP, width)
    partial = jnp.einsum(
        "bts,bsd->btd", combine, expert_out, preferred_element_type=jnp.float32
    ).astype(jnp.bfloat16)
    moe_sum = lax.psum_scatter(
        partial.reshape(groups * shards * rows, width),
        ("dp", "tensor"),
        scatter_dimension=0,
        tiled=True,
    ).astype(jnp.float32)
    combined = mixed_sum + moe_sum
    new_residual = combined.astype(jnp.bfloat16)
    normed = rms_scale(combined, final_gain).astype(jnp.bfloat16)
    return (new_residual, normed, arrived)


def solution(mesh):
    in_specs = (
        P("dp", "tensor"),
        P(("dp", "tensor"), None),
        P("tensor", None),
        P(),
        P(),
        P(("dp", "tensor"), None),
        P("dp", None, None, "tensor"),
        P("dp", "tensor", None),
        P(),
        P("dp", None, "tensor", None),
        P("dp", None),
        P("dp", None),
    )
    out_specs = (
        P(("dp", "tensor"), None),
        P(("dp", "tensor"), None),
        P("dp", None, "tensor", None),
    )
    return jax.shard_map(
        per_device, mesh=mesh, in_specs=in_specs, out_specs=out_specs, check_vma=False
    )
```

```python
import jax
import jax.numpy as jnp
from jax import lax
from jax.experimental import pallas as pl
from jax.experimental.pallas import tpu as pltpu
from jax.sharding import PartitionSpec as P

CAP = 8


def rms_scale(values, gain_vec):
    mean_sq = jnp.mean(values * values, axis=-1, keepdims=True)
    return values * lax.rsqrt(mean_sq + 1e-06) * gain_vec


MESH = pl.DeviceIdType.MESH
EXTRA = 128
F32, BF16 = jnp.float32, jnp.bfloat16


def wide(value):
    return value.astype(F32)


class Place:
    def __init__(self):
        group, shard = lax.axis_index("dp"), lax.axis_index("tensor")
        z, y, x, c = group // 2, group % 2, shard // 2, shard % 2
        self.group, self.z, self.y, self.x, self.c = group, z, y, x, c
        self.planes = [z, z + 1 - 2 * (z % 2), (z + 2) % 4, 3 - z]
        self.core_peer = (group, x * 2 + 1 - c)
        self.x_peer = (group, (1 - x) * 2 + c)
        self.y_peer = (z * 2 + 1 - y, shard)
        self.z_peers = [None] + [(plane * 2 + y, shard) for plane in self.planes[1:]]

    def enter(self):
        barrier = pltpu.get_barrier_semaphore()
        peers = [self.core_peer, self.x_peer, self.y_peer] + self.z_peers[1:]
        for peer in peers:
            pl.semaphore_signal(barrier, inc=1, device_id=peer, device_id_type=MESH)
        pl.semaphore_wait(barrier, len(peers))


def sender(send_sems, recv_sems):
    used = []

    def send(source, target, peer):
        index = len(used)
        copy = pltpu.make_async_remote_copy(
            src_ref=source,
            dst_ref=target,
            send_sem=send_sems.at[index],
            recv_sem=recv_sems.at[index],
            device_id=peer,
            device_id_type=MESH,
        )
        copy.start()
        used.append(copy)
        return copy

    return send, used


def block_kernel(
    pick_ref, target_ref,
    attn_hbm, weight_hbm, residual_hbm, gain_hbm, router_hbm, routes_hbm,
    paired_hbm, down_hbm, kv_hbm,
    combined_ref, arrived_ref,
    attn, weight, residual, gain, router, routes, staged, paired, down, kv,
    made, core_in, x_out, x_in, mixed_ref, everything, slots, combine,
    pick, pick_t, want, want_t, peer_in, first_out, first_in, second_out, second_in, z_out, z_in, pages_in,
    local_sems, stage_sems, send_sems, recv_sems,
):
    at = Place()
    z, y, x, c, planes = at.z, at.y, at.x, at.c, at.planes
    rows, width = residual.shape
    half = width // 2
    experts = paired.shape[0]
    units = down.shape[1]
    loads = {}
    for index, (name, source, target) in enumerate((
        ("attn", attn_hbm, attn), ("weight", weight_hbm, weight), ("kv", kv_hbm, kv),
        ("residual", residual_hbm, residual), ("gain", gain_hbm, gain),
        ("router", router_hbm, router), ("routes", routes_hbm, routes),
        ("down", down_hbm, down),
    )):
        loads[name] = pltpu.make_async_copy(source, target, local_sems.at[index])

    def stage(e):
        return pltpu.make_async_copy(paired_hbm.at[e], staged.at[e % 2], stage_sems.at[e % 2])

    for name in ("attn", "weight", "kv", "residual", "gain", "router", "routes"):
        loads[name].start()
    stage(0).start()
    stage(1).start()
    loads["down"].start()

    def split_pairs(e):
        stage(e).wait()

        def piece(i, carry):
            spot = pl.ds(pl.multiple_of(i * 128, 128), 128)
            both = jnp.swapaxes(staged[e % 2, spot], 0, 1)
            paired[e, spot, :units] = both[0]
            paired[e, spot, units:] = both[1]
            return carry

        lax.fori_loop(0, width // 128, piece, 0)
        if e + 2 < experts:
            stage(e + 2).start()

    at.enter()
    send, used = sender(send_sems, recv_sems)

    loads["kv"].wait()
    for slot in range(2):
        pages_in[z, y, slot, pl.ds(0, 16)] = kv[pick_ref[0, slot]]
        pages_in[z, y, slot, 16] = jnp.full(kv.shape[2:], target_ref[0, slot], jnp.int32).astype(
            F32
        ).astype(BF16)
    own_pages = pages_in.at[z, y]
    page_z = [None] + [send(own_pages, own_pages, at.z_peers[j]) for j in (1, 2, 3)]
    page_y = [send(own_pages, own_pages, at.y_peer)]

    def pass_page(j):
        page_z[j].wait_recv()
        spot = pages_in.at[planes[j], y]
        page_y.append(send(spot, spot, at.y_peer))

    loads["attn"].wait()
    loads["weight"].wait()
    halves = [pl.ds(0, half), pl.ds(half, half)]
    far, near, to_x = [], [], []
    for h in (0, 1):
        for start in range(h * half, h * half + half, 512):
            part = jnp.dot(
                attn[...], weight[:, start : start + 512], preferred_element_type=F32
            )
            for shard in range(4):
                made[shard, :, start : start + 512] = part[
                    shard * rows : (shard + 1) * rows
                ].astype(BF16)
        far.append(
            send(made.at[(1 - x) * 2 + 1 - c, :, halves[h]], core_in.at[0, :, halves[h]], at.core_peer)
        )
    for h in (0, 1):
        near.append(
            send(made.at[x * 2 + 1 - c, :, halves[h]], core_in.at[1, :, halves[h]], at.core_peer)
        )
    for h in (0, 1):
        far[h].wait_recv()
        x_out[:, halves[h]] = (
            wide(made[(1 - x) * 2 + c, :, halves[h]]) + wide(core_in[0, :, halves[h]])
        ).astype(BF16)
        to_x.append(send(x_out.at[:, halves[h]], x_in.at[:, halves[h]], at.x_peer))
    for name, index in WARM:
        {"split": split_pairs, "page": pass_page}[name](index)
    loads["residual"].wait()
    for h in (0, 1):
        near[h].wait_recv()
        mixed_ref[:, halves[h]] = (
            wide(residual[:, halves[h]])
            + wide(made[x * 2 + c, :, halves[h]])
            + wide(core_in[1, :, halves[h]])
        )
    loads["gain"].wait()
    loads["router"].wait()
    loads["routes"].wait()
    count = router.shape[0]
    named = routes[...]
    expert = lax.broadcasted_iota(jnp.int32, (count, rows), 0)
    hits_t = jnp.zeros((count, rows), F32)
    for k in range(named.shape[0]):
        hits_t = hits_t + jnp.where(named[k : k + 1, :] == expert, 1.0, 0.0)
    later = lax.broadcasted_iota(jnp.int32, (rows, rows), 0)
    sooner = lax.broadcasted_iota(jnp.int32, (rows, rows), 1)
    eye = jnp.where(later == sooner, 1.0, 0.0).astype(BF16)
    over_last = (((1,), (1,)), ((), ()))
    hits = lax.dot_general(eye, hits_t.astype(BF16), over_last, preferred_element_type=F32)
    before = jnp.where(later > sooner, 1.0, 0.0).astype(BF16)
    places = hits * (1.0 + jnp.dot(before, hits.astype(BF16), preferred_element_type=F32))
    lanes = 2 * CAP
    span = experts * lanes
    first_expert = at.group * experts

    def iota(shape, axis):
        return lax.broadcasted_iota(jnp.int32, shape, axis)

    def wanted(slot, token):
        return wide(jnp.where(slot // CAP % 2 == token // rows, slot % CAP + 1, -1))

    def picks(slot, entry):
        chosen = first_expert + slot % span // lanes + slot // span * count
        return jnp.where(chosen == entry, 1.0, 0.0).astype(BF16)

    tall, square = (2 * span, 2 * count), (span, 2 * rows)
    pick_t[...] = picks(iota(tall, 0), iota(tall, 1))
    pick[...] = picks(iota(tall[::-1], 1), iota(tall[::-1], 0))
    want_t[...] = wanted(iota(square, 0), iota(square, 1))
    want[...] = wanted(iota(square[::-1], 1), iota(square[::-1], 0))
    to_x[0].wait_recv()
    to_x[1].wait_recv()
    mixed = mixed_ref[...] + wide(x_in[...])
    mixed_ref[...] = mixed
    mean_sq = jnp.mean(mixed * mixed, axis=-1, keepdims=True)
    rounded = (mixed * lax.rsqrt(mean_sq + 1e-06) * gain[...]).astype(BF16)
    everything[z, y, x, c, :, :width] = rounded
    logits = lax.dot_general(rounded, router[...], over_last, preferred_element_type=F32)
    gates = jax.nn.sigmoid(logits)
    everything[z, y, x, c, :, width:] = jnp.concatenate([gates * hits, places], axis=1).astype(
        BF16
    )

    columns = [pl.ds(0, half), pl.ds(half, half + EXTRA)]
    first_peer, second_peer = [at.y_peer, at.x_peer], [at.x_peer, at.y_peer]

    def block(h, j, first_other, second_other):
        ys = first_other if h == 0 else second_other
        xs = second_other if h == 0 else first_other
        return everything.at[
            planes[j], 1 - y if ys else y, 1 - x if xs else x, c, :, columns[h]
        ]

    z_copies, first_copies, second_copies = {}, {}, {}
    core_copies = {j: [] for j in range(4)}
    sent = {j: [] for j in range(4)}

    def note(j, copy):
        sent[j].append(copy)
        return copy

    def core(j, spot):
        core_copies[j].append(note(j, send(spot, spot, at.core_peer)))

    def send_z(j):
        for h in (0, 1):
            spot = block(h, 0, 0, 0)
            z_copies[h, j] = note(0, send(spot, spot, at.z_peers[j]))

    def spread(j):
        for h in (0, 1):
            if j:
                z_copies[h, j].wait_recv()
            spot = block(h, j, 0, 0)
            first_copies[h, j] = note(j, send(spot, spot, first_peer[h]))
        for h in (0, 1):
            spot = block(h, j, 0, 0)
            second_copies[h, j, 0] = note(j, send(spot, spot, second_peer[h]))
        for h in (0, 1):
            core(j, block(h, j, 0, 0))

    def spread_first(j):
        for h in (0, 1):
            first_copies[h, j].wait_recv()
            spot = block(h, j, 1, 0)
            second_copies[h, j, 1] = note(j, send(spot, spot, second_peer[h]))
        for h in (0, 1):
            core(j, block(h, j, 1, 0))

    def spread_second(j):
        for other in (0, 1):
            for h in (0, 1):
                second_copies[h, j, other].wait_recv()
                core(j, block(h, j, other, 1))

    def dispatch(j):
        for copy in core_copies[j]:
            copy.wait_recv()

        def one_chip(i, carry):
            spot = everything.at[planes[j], i // 2, i % 2]
            tail = spot[:, :, width:].reshape(2 * rows, EXTRA)
            seats = lax.dot_general(pick_t[span:], tail, over_last, preferred_element_type=F32)
            table = jnp.where(seats == want_t[...], 1.0, 0.0).astype(BF16)
            local = jnp.dot(tail, pick[...], preferred_element_type=F32)
            combine[j, i] = jnp.where(local[:, span:] == want[...], local[:, :span], 0.0)
            packed = jnp.dot(
                table,
                spot[:, :, :width].reshape(2 * rows, width),
                preferred_element_type=F32,
            ).astype(BF16)
            for e in range(experts):
                slots[e, PLACE[j], pl.ds(pl.multiple_of(i * lanes, lanes), lanes), :] = packed[
                    e * lanes : (e + 1) * lanes
                ]
            return carry

        lax.fori_loop(0, 4, one_chip, 0)

    def feed(first_place, count_planes, first, last):
        here = pl.ds(first_place, count_planes)
        seats = slots.shape[2]

        def one_expert(e, carry):
            taken = slots[e, here].reshape(count_planes * seats, width)
            both = jnp.dot(taken, paired[e], preferred_element_type=F32)
            gate, up = both[:, :units], both[:, units:]
            hidden = (gate / (1.0 + jnp.exp(-gate)) * up).astype(BF16)
            for start in range(0, width, 512):
                out = jnp.dot(
                    hidden, down[e, :, start : start + 512], preferred_element_type=F32
                ).astype(BF16)
                slots[e, here, :, start : start + 512] = out.reshape(count_planes, seats, 512)
            return carry

        for e in range(first, last):
            one_expert(e, 0)

    peer_copies, first_sums, second_sums, z_sums = {}, {}, {}, {}
    orders = ((1, 1), (0, 1), (1, 0), (0, 0))

    def owner(j, fy, fx, core_id, h=None):
        cut = pl.ds(0, width) if h is None else halves[h]
        return (planes[j], 1 - y if fy else y, 1 - x if fx else x, core_id, slice(None), cut)

    def gather_sums(j):
        for copy in sent[j]:
            copy.wait_send()

        for turn, (fy, fx) in enumerate(orders):
            ys, xs = 1 - y if fy else y, 1 - x if fx else x
            i = ys * 2 + xs
            spot = pl.ds(pl.multiple_of(i * lanes, lanes), lanes)

            def piece(k, carry):
                cut = pl.ds(pl.multiple_of(k * 512, 512), 512)
                outs = jnp.concatenate(
                    [slots[e, PLACE[j], spot, cut] for e in range(experts)], axis=0
                )
                part = jnp.dot(combine[j, i].astype(BF16), outs, preferred_element_type=F32)
                for core_id in (0, 1):
                    everything[planes[j], ys, xs, core_id, :, cut] = part[
                        core_id * rows : (core_id + 1) * rows
                    ].astype(BF16)
                return carry

            lax.fori_loop(0, width // 512, piece, 0, unroll=True)
            peer_copies[j, fy, fx] = send(
                everything.at[owner(j, fy, fx, 1 - c)], peer_in.at[j, fy, fx], at.core_peer
            )
            if turn >= LAG:
                pass_first(j, *orders[turn - LAG])

    def both_cores(j, fy, fx, h):
        return wide(everything[owner(j, fy, fx, c, h)]) + wide(peer_in[j, fy, fx, :, halves[h]])

    def pass_first(j, fy, fx):
        peer_copies[j, fy, fx].wait_recv()
        for h in (0, 1):
            across, second = ((fx, fy), (fy, fx))[h]
            if across:
                first_out[j, h, second] = both_cores(j, fy, fx, h).astype(BF16)
                first_sums[j, h, second] = send(
                    first_out.at[j, h, second],
                    first_in.at[j, h, second],
                    (at.x_peer, at.y_peer)[h],
                )

    def sum_first(j):
        for fy, fx in orders[4 - LAG : 3]:
            pass_first(j, fy, fx)

    def sum_second(j):
        for h in (0, 1):
            first_sums[j, h, 1].wait_recv()
            fy, fx = (1, 0) if h == 0 else (0, 1)
            second_out[j, h] = (both_cores(j, fy, fx, h) + wide(first_in[j, h, 1])).astype(BF16)
            second_sums[j, h] = send(
                second_out.at[j, h], second_in.at[j, h], (at.y_peer, at.x_peer)[h]
            )

    def sum_plane(j):
        peer_copies[j, 0, 0].wait_recv()
        for h in (0, 1):
            first_sums[j, h, 0].wait_recv()
            second_sums[j, h].wait_recv()
            total = both_cores(j, 0, 0, h) + wide(first_in[j, h, 0]) + wide(second_in[j, h])
            if j:
                z_out[j - 1, h] = total.astype(BF16)
                z_sums[j, h] = send(z_out.at[j - 1, h], z_in.at[j - 1, h], at.z_peers[j])
            else:
                mixed_ref[:, halves[h]] = mixed_ref[:, halves[h]] + total

    def pages_out():
        for copy in page_y:
            copy.wait_recv()
        me = at.group.astype(F32)
        for slot in range(2):
            found = jnp.zeros(arrived_ref.shape[1:], F32)
            for zs in range(4):
                for ys in (0, 1):
                    held = wide(pages_in[zs, ys, slot])
                    found = found + jnp.where(held[16:17] == me, held[:16], 0.0)
            arrived_ref[slot] = found.astype(BF16)

    def finish():
        for h in (0, 1):
            value = mixed_ref[:, halves[h]]
            for j in Z_ORDER:
                z_sums[j, h].wait_recv()
                value = value + wide(z_in[j - 1, h])
            combined_ref[:, halves[h]] = value

    steps = dict(
        z=send_z, spread=spread, first=spread_first, second=spread_second, dispatch=dispatch,
        split=split_pairs, feed=feed, down=loads["down"].wait, sums=gather_sums, one=sum_first,
        two=sum_second, plane=sum_plane, pages=pages_out, finish=finish, page=pass_page,
    )
    for name, *given in SCHEDULE:
        steps[name](*given)
    waited = {id(copy) for j in range(4) for copy in sent[j]}
    for copy in used:
        if id(copy) not in waited:
            copy.wait_send()


PLACE = (0, 2, 1, 3)
Z_ORDER = (2, 3, 1)
LAG = 4
WARM = (("split", 0), ("split", 1), ("page", 1), ("split", 2), ("page", 2), ("page", 3), ("split", 3))
SCHEDULE = (
    ("z", 2), ("spread", 0), ("z", 1), ("first", 0), ("split", 4), ("spread", 2), ("z", 3),
    ("split", 5), ("second", 0), ("first", 2), ("split", 6), ("split", 7), ("spread", 1),
    ("dispatch", 0), ("second", 2), ("first", 1), ("dispatch", 2), ("down",), ("spread", 3),
    ("feed", 0, 2, 0, 4), ("second", 1), ("feed", 0, 2, 4, 8), ("first", 3), ("second", 3),
    ("sums", 2), ("dispatch", 1), ("one", 2), ("sums", 0), ("dispatch", 3), ("one", 0),
    ("feed", 2, 2, 0, 6), ("two", 2), ("two", 0), ("feed", 2, 2, 6, 8), ("sums", 3),
    ("plane", 2), ("sums", 1), ("one", 3), ("two", 3), ("one", 1), ("pages",), ("plane", 3),
    ("two", 1), ("plane", 1), ("plane", 0), ("finish",),
)
COPIES = 3 + 4 + 6 + 2 * (3 + 4 + 8 + 16) + 16 + 16 + 8 + 6


def close_kernel(
    combined_hbm, gain_hbm, arrived_hbm, new_hbm, normed_hbm, out_hbm,
    combined, gain, new, normed, pages, sems,
):
    copies = [
        pltpu.make_async_copy(source, target, sems.at[index])
        for index, (source, target) in enumerate((
            (combined_hbm, combined), (gain_hbm, gain), (arrived_hbm, pages),
            (new, new_hbm), (normed, normed_hbm), (pages, out_hbm),
        ))
    ]
    for copy in copies[:3]:
        copy.start()
    copies[0].wait()
    value = combined[...]
    new[...] = value.astype(BF16)
    copies[3].start()
    copies[1].wait()
    scale = lax.rsqrt(jnp.mean(value * value, axis=-1, keepdims=True) + 1e-06)
    normed[...] = (value * scale * gain[...]).astype(BF16)
    copies[4].start()
    copies[2].wait()
    copies[5].start()
    for copy in copies[3:]:
        copy.wait()


def close(combined, gain, arrived):
    hbm = pl.BlockSpec(memory_space=pl.ANY)
    kept = jax.ShapeDtypeStruct(combined.shape, BF16)
    scratch = lambda value: pltpu.VMEM(value.shape, value.dtype)
    return pl.pallas_call(
        close_kernel,
        out_shape=(kept, kept, jax.ShapeDtypeStruct(arrived.shape, BF16)),
        in_specs=[hbm] * 3,
        out_specs=(hbm,) * 3,
        scratch_shapes=[scratch(v) for v in (combined, gain, kept, kept, arrived)]
        + [pltpu.SemaphoreType.DMA((6,))],
        name="close",
    )(combined, gain, arrived)


def whole_block(
    attn_out, out_weight, residual, norm_gain, router_weight, routes, gate_up, down_weight,
    final_gain, kv_pages, page_pick, destination,
):
    rows, width = residual.shape
    half = width // 2
    experts, _, _, units = gate_up.shape
    hbm, smem, vmem = (
        pl.BlockSpec(memory_space=space) for space in (pl.ANY, pltpu.SMEM, pltpu.VMEM)
    )
    scratch = lambda value: pltpu.VMEM(value.shape, value.dtype)
    blocks = lambda *shape: pltpu.VMEM(shape, BF16)
    page = kv_pages.shape[1:]
    gain = norm_gain.reshape(1, width)
    router, named = router_weight.T, routes.T
    combined, arrived = pl.pallas_call(
        block_kernel,
        out_shape=(
            jax.ShapeDtypeStruct((rows, width), F32),
            jax.ShapeDtypeStruct((2,) + page, BF16),
        ),
        in_specs=[smem] * 2 + [hbm] * 9,
        out_specs=(vmem,) * 2,
        scratch_shapes=[
            scratch(attn_out), scratch(out_weight), scratch(residual), scratch(gain),
            scratch(router), scratch(named),
            blocks(2, width, 2, units),
            blocks(experts, width, 2 * units),
            scratch(down_weight), scratch(kv_pages),
            blocks(4, rows, width),
            blocks(2, rows, width),
            blocks(rows, width),
            blocks(rows, width),
            pltpu.VMEM((rows, width), F32),
            blocks(4, 2, 2, 2, rows, width + EXTRA),
            blocks(experts, 4, 4 * 2 * CAP, width),
            pltpu.VMEM((4, 4, 2 * rows, experts * 2 * CAP), F32),
            blocks(2 * router_weight.shape[1], 2 * experts * 2 * CAP),
            blocks(2 * experts * 2 * CAP, 2 * router_weight.shape[1]),
            pltpu.VMEM((2 * rows, experts * 2 * CAP), F32),
            pltpu.VMEM((experts * 2 * CAP, 2 * rows), F32),
            blocks(4, 2, 2, rows, width),
            blocks(4, 2, 2, rows, half),
            blocks(4, 2, 2, rows, half),
            blocks(4, 2, rows, half),
            blocks(4, 2, rows, half),
            blocks(3, 2, rows, half),
            blocks(3, 2, rows, half),
            blocks(4, 2, 2, page[0] + 1, page[1], page[2]),
            pltpu.SemaphoreType.DMA((8,)),
            pltpu.SemaphoreType.DMA((2,)),
            pltpu.SemaphoreType.DMA((COPIES,)),
            pltpu.SemaphoreType.DMA((COPIES,)),
        ],
        compiler_params=pltpu.CompilerParams(
            collective_id=0, has_side_effects=True, vmem_limit_bytes=60 << 20
        ),
        name="block",
    )(
        page_pick, destination, attn_out, out_weight, residual, gain, router, named,
        gate_up, down_weight, kv_pages,
    )
    return close(combined, final_gain.reshape(1, width), arrived)


def pair_kernel(taken_ref, paired_ref, out_ref):
    units = paired_ref.shape[3]
    both = jnp.swapaxes(paired_ref[0], 0, 1)
    for part in (0, 1):
        out_ref[0, :, part * units : (part + 1) * units] = jnp.dot(
            taken_ref[0], both[part], preferred_element_type=F32
        )


def pair_products(taken, gate_up):
    experts, count, width = taken.shape
    units = gate_up.shape[3]
    step = 256 if count % 256 == 0 else count
    return pl.pallas_call(
        pair_kernel,
        grid=(experts, count // step),
        out_shape=jax.ShapeDtypeStruct((experts, count, 2 * units), F32),
        in_specs=[
            pl.BlockSpec((1, step, width), lambda e, i: (e, i, 0)),
            pl.BlockSpec((1, width, 2, units), lambda e, i: (e, 0, 0, 0)),
        ],
        out_specs=pl.BlockSpec((1, step, 2 * units), lambda e, i: (e, i, 0)),
        compiler_params=pltpu.CompilerParams(vmem_limit_bytes=32 << 20),
        name="pair",
    )(taken, gate_up)


def migrate(kv_pages, page_pick, destination):
    groups = lax.axis_size("dp")
    chosen_pages = jnp.concatenate(
        [
            lax.dynamic_slice_in_dim(kv_pages, page_pick[0, slot], 1, axis=0)
            for slot in range(page_pick.shape[1])
        ],
        axis=0,
    )
    owners = jnp.arange(groups, dtype=jnp.int32)[:, None] == destination[0][None, :]
    outgoing = jnp.where(
        owners[:, :, None, None, None], chosen_pages[None], jnp.zeros((), kv_pages.dtype)
    )
    incoming = lax.all_to_all(outgoing, "dp", split_axis=0, concat_axis=0, tiled=True)
    return jnp.sum(incoming, axis=0)


def local_slots(routes_all, first, local_experts, groups, shards, rows):
    hits = jnp.any(
        routes_all[:, :, None] == first + jnp.arange(local_experts, dtype=jnp.int32), axis=1
    )
    hits = hits.reshape(groups, shards * rows, local_experts)
    token = jnp.arange(shards * rows, dtype=jnp.int32)
    before = (token[:, None] > token[None, :]) & (
        token[:, None] // rows == token[None, :] // rows
    )
    rank = jnp.einsum(
        "ut,bte->bue",
        before.astype(jnp.bfloat16),
        hits.astype(jnp.bfloat16),
        preferred_element_type=jnp.float32,
    ).astype(jnp.int32)
    within = (token // rows * CAP)[None, :, None] + rank
    within = jnp.where(hits, within, -1)
    slots = jnp.arange(shards * CAP, dtype=jnp.int32)
    table = within[:, :, :, None] == slots
    return table.reshape(groups, shards * rows, local_experts * shards * CAP)


def per_device(
    attn_out,
    residual,
    out_weight,
    norm_gain,
    router_weight,
    routes,
    gate_up,
    down_weight,
    final_gain,
    kv_pages,
    page_pick,
    destination,
):
    groups = lax.axis_size("dp")
    shards = lax.axis_size("tensor")
    rows, width = residual.shape
    local_experts = gate_up.shape[0]
    first = lax.axis_index("dp") * local_experts
    if groups == 8 and shards == 4:
        return whole_block(
            attn_out, out_weight, residual, norm_gain, router_weight, routes, gate_up,
            down_weight, final_gain, kv_pages, page_pick, destination,
        )
    arrived = migrate(kv_pages, page_pick, destination)
    routes_all = lax.all_gather(routes, ("dp", "tensor"), axis=0, tiled=True)
    projected = lax.psum_scatter(
        jnp.dot(attn_out, out_weight, preferred_element_type=jnp.float32).astype(
            jnp.bfloat16
        ),
        "tensor",
        scatter_dimension=0,
        tiled=True,
    ).astype(jnp.float32)
    mixed_sum = residual.astype(jnp.float32) + projected
    normed_in = rms_scale(mixed_sum, norm_gain).astype(jnp.bfloat16)
    tokens = lax.all_gather(normed_in, ("dp", "tensor"), axis=0, tiled=True)
    table = local_slots(routes_all, first, local_experts, groups, shards, rows)
    local_router = lax.dynamic_slice_in_dim(router_weight, first, local_experts, axis=1)
    logits = jnp.dot(tokens, local_router, preferred_element_type=jnp.float32)
    gates = jax.nn.sigmoid(logits).astype(jnp.bfloat16)
    tokens = tokens.reshape(groups, shards * rows, width)
    gates = jnp.repeat(
        gates.reshape(groups, shards * rows, local_experts), shards * CAP, axis=2
    )
    placement = table.astype(jnp.bfloat16)
    combine = jnp.where(table, gates, jnp.zeros((), jnp.bfloat16))
    slotted = jnp.einsum(
        "bts,btd->bsd", placement, tokens, preferred_element_type=jnp.float32
    ).astype(jnp.bfloat16)
    slotted = slotted.reshape(groups, local_experts, shards * CAP, width)
    units = gate_up.shape[3]
    taken = jnp.swapaxes(slotted, 0, 1).reshape(local_experts, -1, width)
    paired = pair_products(taken, gate_up)
    paired = jnp.swapaxes(paired.reshape(local_experts, groups, shards * CAP, 2 * units), 0, 1)
    hidden = (jax.nn.silu(paired[..., :units]) * paired[..., units:]).astype(jnp.bfloat16)
    expert_out = jnp.einsum(
        "becf,efd->becd", hidden, down_weight, preferred_element_type=jnp.float32
    ).astype(jnp.bfloat16)
    expert_out = expert_out.reshape(groups, local_experts * shards * CAP, width)
    partial = jnp.einsum(
        "bts,bsd->btd", combine, expert_out, preferred_element_type=jnp.float32
    ).astype(jnp.bfloat16)
    moe_sum = lax.psum_scatter(
        partial.reshape(groups * shards * rows, width),
        ("dp", "tensor"),
        scatter_dimension=0,
        tiled=True,
    ).astype(jnp.float32)
    combined = mixed_sum + moe_sum
    new_residual = combined.astype(jnp.bfloat16)
    normed = rms_scale(combined, final_gain).astype(jnp.bfloat16)
    return (new_residual, normed, arrived)


def solution(mesh):
    in_specs = (
        P("dp", "tensor"),
        P(("dp", "tensor"), None),
        P("tensor", None),
        P(),
        P(),
        P(("dp", "tensor"), None),
        P("dp", None, None, "tensor"),
        P("dp", "tensor", None),
        P(),
        P("dp", None, "tensor", None),
        P("dp", None),
        P("dp", None),
    )
    out_specs = (
        P(("dp", "tensor"), None),
        P(("dp", "tensor"), None),
        P("dp", None, "tensor", None),
    )
    return jax.shard_map(
        per_device, mesh=mesh, in_specs=in_specs, out_specs=out_specs, check_vma=False
    )
```
